256 devices in a mesh: row: 64 (over y, z, core), col: 4 (over x).
Axes of the slice: x: 4, y: 4, z: 8, core: 2. Of those that a mesh axis runs over, the one named last changes fastest.
Arguments:
- green: bfloat16 [8192, 5, 8192], P('col', None, 'row'), as said below
- arrival: int32 [1200, 5, 64], P(None, None, 'row'), may hold values from 512 to 3071
- row_gauge: int32 [8192], P('col'), may hold values from 0 to 1199
- row_time: int32 [8192], P('col'), may hold values from 0 to 4095, as said below
- damping: float32 [512], replicated, may hold values from 0.5 to 2
- trail: float32 [5, 8192, 8, 512], P(None, 'row', None, 'col'), may hold values from -0.4 to 0.4
Outputs:
- chol_panel: float32 [5, 8192, 512], P(None, 'row', 'col')
- trail_out: float32 [5, 8192, 8, 512], P(None, 'row', None, 'col')
The draws below stay inside these ranges and needn't reach their ends.
Inputs may be any that keep to these rules, and one draw needn't show every extreme that they name: `row_time`: nondecreasing along the rows; the first row has time 0 and the last row time 4096 - 1. `green`: real-valued entries of order 2048 ** -0.5.
All inputs are finite; a program needn't handle non-finite values.
Results may differ from the reference program's by a relative error of at most 0.0003.
Values may be sent and summed in bfloat16 or wider, within the bound.
A program may use at most 64 MiB of HBM per device.

```python
import math
import jax
import jax.numpy as jnp
from jax import lax

NB = 128
PANEL = 512
TRAIL = 4096
RT_DEV = 5
GAUGES = 1200
SAMPLES = 4096
KQ = 2048
K = 8192
ORDER = 40960
N_ROW = 64
N_COL = 4


def draw_row_time(key, part):
    values = jnp.sort(jax.random.randint(key, (K,), 0, SAMPLES))
    values = values.at[0].set(0).at[K - 1].set(SAMPLES - 1)
    return values.astype(jnp.int32)


def draw_green(key, part):
    key_common = jax.random.fold_in(key, 11)
    key_own = jax.random.fold_in(key, 12)
    key_load = jax.random.fold_in(key, 13)
    common = jnp.clip(jax.random.normal(key_common, (K, RT_DEV, N_ROW, 1), jnp.float32), -4.0, 4.0)
    own = jnp.clip(jax.random.normal(key_own, (K, RT_DEV, N_ROW * NB), jnp.float32), -4.0, 4.0)
    load = jax.random.uniform(key_load, (1, RT_DEV, N_ROW * NB), jnp.float32, 0.55, 0.9)
    common = jnp.broadcast_to(common, (K, RT_DEV, N_ROW, NB)).reshape(K, RT_DEV, N_ROW * NB)
    values = (load * common + jnp.sqrt(1.0 - load * load) * own) * float(KQ) ** (-0.5)
    return values.astype(jnp.bfloat16)


def plant(array, stream_key, low, high):
    shape = array.shape
    index_at = [jax.random.randint(jax.random.fold_in(stream_key, axis), (), 0, shape[axis]) for axis in range(len(shape))]
    array = array.at[tuple(index_at)].set(low)
    longest = shape.index(max(shape))
    index_at[longest] = (index_at[longest] + 1) % shape[longest]
    return array.at[tuple(index_at)].set(high)


def block_scale(own_key, extent, cuts, low, largest):
    factor_of = 1.0
    for axis_at, shards_of in cuts:
        heights = jax.random.uniform(jax.random.fold_in(jax.random.fold_in(own_key, 6), axis_at), (shards_of,), jnp.float32, low / len(cuts), largest / len(cuts))
        factor_of = factor_of * jnp.repeat(jnp.exp(heights), extent[axis_at] // shards_of).reshape((-1,) + (1,) * (len(extent) - 1 - axis_at))
    return factor_of


def scatter_about(rng, extent, spread, limit, cuts=(), kind=jnp.bfloat16):
    array = spread * jax.random.normal(rng, extent, jnp.float32)
    if cuts:
        array = array * block_scale(rng, extent, cuts, -0.22, 0.18)
    return jnp.clip(array, -limit, limit).astype(kind)


def setup_inputs(seed: int = 0) -> dict:
    key_of = jax.random.split(jax.random.key(seed), 7)
    green = draw_green(jax.random.fold_in(key_of[6], 71), 0)
    arrival = plant(jax.random.randint(key_of[1], (GAUGES, RT_DEV, N_ROW), SAMPLES // 8, SAMPLES * 3 // 4), jax.random.fold_in(key_of[1], 1), SAMPLES // 8, (SAMPLES * 3 // 4) - 1).astype(jnp.int32)
    row_gauge = plant(jax.random.randint(key_of[2], (K,), 0, GAUGES), jax.random.fold_in(key_of[2], 1), 0, GAUGES - 1).astype(jnp.int32)
    row_time = draw_row_time(jax.random.fold_in(key_of[6], 71), 0)
    damping = jnp.clip(jnp.exp(jax.random.uniform(key_of[4], (PANEL,), jnp.float32, math.log(0.5), math.log(2.0))), 0.5, 2.0)
    trail = scatter_about(key_of[5], (RT_DEV, N_ROW * NB, TRAIL // NB // N_COL, N_COL * NB), 0.05, 0.4, ((1, 64), (3, 4)), jnp.float32)
    return {"green": green, "arrival": arrival, "row_gauge": row_gauge, "row_time": row_time, "damping": damping, "trail": trail}


def reference(green, arrival, row_gauge, row_time, damping, trail):
    tile_count = RT_DEV * N_ROW
    panel_tiles = PANEL // NB
    arrive_grid = arrival.reshape(GAUGES, RT_DEV, N_ROW)
    is_live = row_time[:, None, None] >= arrive_grid[row_gauge]
    panel_source = green.reshape(K, tile_count, NB)[:, :panel_tiles]
    panel_live = is_live.reshape(K, tile_count)[:, :panel_tiles]
    panel_cols = jnp.where(panel_live[:, :, None], panel_source, jnp.zeros_like(panel_source)).reshape(K, PANEL)

    def group_rows(index_no):
        source = lax.dynamic_index_in_dim(green, index_no, 1, keepdims=False).reshape(K, N_ROW, NB)
        alive = lax.dynamic_index_in_dim(is_live, index_no, 1, keepdims=False)
        masked = jnp.where(alive[:, :, None], source, jnp.zeros_like(source)).reshape(K, N_ROW * NB)
        return lax.dot_general(masked.astype(jnp.float32), panel_cols.astype(jnp.float32), (((0,), (0,)), ((), ())), preferred_element_type=jnp.float32)
    normal_rows = lax.map(group_rows, jnp.arange(RT_DEV, dtype=jnp.int32)).reshape(ORDER, PANEL)
    factor = jnp.linalg.cholesky(normal_rows[:PANEL] + jnp.diag(damping))
    solved = lax.linalg.triangular_solve(factor, normal_rows, left_side=False, lower=True, transpose_a=True)
    lower_rows = solved.at[:PANEL].set(factor)
    far_rows = lower_rows[PANEL:PANEL + TRAIL]
    update = jnp.dot(lower_rows.astype(jnp.float32), far_rows.T.astype(jnp.float32), precision=lax.Precision.HIGHEST, preferred_element_type=jnp.float32)
    target = trail.reshape(ORDER, TRAIL)
    below_panel = (jnp.arange(ORDER, dtype=jnp.int32) >= PANEL)[:, None]
    result = target - jnp.where(below_panel, update, jnp.zeros_like(update))
    return (lower_rows.reshape(RT_DEV, N_ROW * NB, PANEL), result.reshape(RT_DEV, N_ROW * NB, TRAIL // NB // N_COL, N_COL * NB))
```

```python
import numpy as np
import jax
import jax.numpy as jnp
from jax import lax
from jax.sharding import PartitionSpec as P

NB = 128
PANEL = 512


def tree_share(piece, holds, spread_masks, gather_masks, row_count, col_count):
    row_pos = lax.axis_index("row")
    col_pos = lax.axis_index("col")
    flat_pos = row_pos * col_count + col_pos
    have = np.array(holds, dtype=bool)
    for mask in spread_masks:
        pairs = []
        gets = np.zeros_like(have)
        for r in range(row_count):
            for c in range(col_count):
                if have[r, c] and not have[r ^ mask, c]:
                    pairs.append((r * col_count + c, (r ^ mask) * col_count + c))
                    gets[r ^ mask, c] = True
        moved = lax.ppermute(piece, ("row", "col"), pairs)
        took = jnp.asarray(gets.reshape(-1))[flat_pos]
        piece = jnp.where(took, moved, piece)
        have = have | gets
    assert have.all()
    for mask in gather_masks:
        pairs = [
            (r * col_count + c, (r ^ mask) * col_count + c)
            for r in range(row_count)
            for c in range(col_count)
        ]
        other = lax.ppermute(piece, ("row", "col"), pairs)
        upper = (row_pos & mask) != 0
        low = jnp.where(upper, other, piece)
        high = jnp.where(upper, piece, other)
        piece = jnp.stack([low, high])
    return piece


def local(green, arrival, row_gauge, row_time, damping, trail):
    row_count = lax.axis_size("row")
    col_count = lax.axis_size("col")
    row_pos = lax.axis_index("row")
    col_pos = lax.axis_index("col")
    kq_rows, tile_rows, tile_width = green.shape
    panel_tiles = PANEL // NB
    far_slots = trail.shape[2]
    arrive = arrival[row_gauge][:, :, 0]
    is_live = row_time[:, None] >= arrive
    masked = jnp.where(is_live[:, :, None], green, jnp.zeros_like(green))
    flat_green = masked.reshape(kq_rows, tile_rows * tile_width)

    panel_holds = np.zeros((row_count, col_count), dtype=bool)
    panel_holds[:panel_tiles, :] = True
    shared = tree_share(
        masked[:, 0, :], panel_holds, (8, 32, 4, 16), (2, 1), row_count, col_count
    )
    panel_stack = jnp.transpose(shared, (1, 0, 2, 3)).reshape(panel_tiles, kq_rows, tile_width)
    panel_cols = jnp.transpose(panel_stack, (1, 0, 2)).reshape(kq_rows, PANEL)

    contract_rows = (((0,), (0,)), ((), ()))
    diag_part = lax.dot_general(
        panel_cols, panel_cols, contract_rows, preferred_element_type=jnp.float32
    )
    partial_value = lax.dot_general(
        flat_green, panel_cols, contract_rows, preferred_element_type=jnp.float32
    )
    diag_block = lax.psum(diag_part, "col")
    normal_rows = lax.psum(partial_value, "col")
    factor = jnp.linalg.cholesky(diag_block + jnp.diag(damping))
    solved = lax.linalg.triangular_solve(
        factor, normal_rows, left_side=False, lower=True, transpose_a=True
    )
    solved = solved.reshape(tile_rows, tile_width, PANEL)
    tiles_list = []
    for local_no in range(tile_rows):
        tile_id = local_no * row_count + row_pos
        diag_rows = lax.dynamic_slice_in_dim(
            factor, jnp.minimum(tile_id, panel_tiles - 1) * tile_width, tile_width, 0
        )
        tiles_list.append(jnp.where(tile_id < panel_tiles, diag_rows, solved[local_no]))
    lower_rows = jnp.stack(tiles_list)
    col_share = PANEL // col_count
    chol_out = lax.dynamic_slice_in_dim(lower_rows, col_pos * col_share, col_share, 2)

    far_holds = np.zeros((row_count, col_count), dtype=bool)
    for slot_no in range(far_slots):
        for c in range(col_count):
            far_holds[panel_tiles + slot_no * col_count + c, c] = True
    far_shared = tree_share(
        lower_rows[0], far_holds, (32, 2, 1), (8, 4, 16), row_count, col_count
    )
    by_value = jnp.transpose(far_shared, (0, 2, 1, 3, 4)).reshape(far_slots, tile_width, PANEL)
    far_rows = jnp.roll(by_value, -1, axis=0).reshape(far_slots * tile_width, PANEL)
    update = lax.dot_general(
        lower_rows.reshape(tile_rows * tile_width, PANEL),
        far_rows,
        (((1,), (1,)), ((), ())),
        precision=lax.Precision.HIGHEST,
        preferred_element_type=jnp.float32,
    )
    update = update.reshape(tile_rows, tile_width, far_slots, tile_width)
    tile_ids = jnp.arange(tile_rows, dtype=jnp.int32) * row_count + row_pos
    below_panel = (tile_ids >= panel_tiles)[:, None, None, None]
    return (chol_out, trail - jnp.where(below_panel, update, jnp.zeros_like(update)))


def solution(mesh):
    return jax.shard_map(
        local,
        mesh=mesh,
        in_specs=(
            P("col", None, "row"),
            P(None, None, "row"),
            P("col"),
            P("col"),
            P(),
            P(None, "row", None, "col"),
        ),
        out_specs=(P(None, "row", "col"), P(None, "row", None, "col")),
        check_vma=False,
    )
```

```python
import numpy as np
import jax
import jax.numpy as jnp
from jax import lax
from jax.sharding import PartitionSpec as P

NB = 128
PANEL = 512


def span_of(masks):
    values = [0]
    for mask in masks:
        values = values + [v ^ mask for v in values]
    return values


def tree_share(piece, holds, spread_rounds, gather_masks, row_count, col_count):
    row_pos = lax.axis_index("row")
    col_pos = lax.axis_index("col")
    flat_pos = row_pos * col_count + col_pos
    have = np.array(holds, dtype=bool)
    for round_masks in spread_rounds:
        gets_all = np.zeros_like(have)
        moved_list = []
        for mask in span_of(round_masks)[1:]:
            pairs = []
            gets = np.zeros_like(have)
            for r in range(row_count):
                for c in range(col_count):
                    if have[r, c] and not have[r ^ mask, c]:
                        pairs.append((r * col_count + c, (r ^ mask) * col_count + c))
                        gets[r ^ mask, c] = True
            assert not (gets & gets_all).any()
            gets_all = gets_all | gets
            moved_list.append((lax.ppermute(piece, ("row", "col"), pairs), gets))
        for moved, gets in moved_list:
            took = jnp.asarray(gets.reshape(-1))[flat_pos]
            piece = jnp.where(took, moved, piece)
        have = have | gets_all
    assert have.all()
    offsets = span_of(gather_masks)
    recv = [piece]
    for mask in offsets[1:]:
        pairs = [
            (r * col_count + c, (r ^ mask) * col_count + c)
            for r in range(row_count)
            for c in range(col_count)
        ]
        recv.append(lax.ppermute(piece, ("row", "col"), pairs))
    stacked = jnp.stack(recv)
    own_value = sum(
        jnp.where((row_pos & mask) != 0, 1 << bit, 0) for bit, mask in enumerate(gather_masks)
    )
    return jnp.stack(
        [lax.dynamic_index_in_dim(stacked, u ^ own_value, 0, keepdims=False) for u in range(len(offsets))]
    )


def local(green, arrival, row_gauge, row_time, damping, trail):
    row_count = lax.axis_size("row")
    col_count = lax.axis_size("col")
    row_pos = lax.axis_index("row")
    col_pos = lax.axis_index("col")
    kq_rows, tile_rows, tile_width = green.shape
    panel_tiles = PANEL // NB
    far_slots = trail.shape[2]
    arrive = arrival[row_gauge][:, :, 0]
    is_live = row_time[:, None] >= arrive
    masked = jnp.where(is_live[:, :, None], green, jnp.zeros_like(green))
    flat_green = masked.reshape(kq_rows, tile_rows * tile_width)

    panel_holds = np.zeros((row_count, col_count), dtype=bool)
    panel_holds[:panel_tiles, :] = True
    panel_stack = tree_share(
        masked[:, 0, :], panel_holds, ((4, 8), (16, 32)), (1, 2), row_count, col_count
    )
    panel_cols = jnp.transpose(panel_stack, (1, 0, 2)).reshape(kq_rows, PANEL)

    contract_rows = (((0,), (0,)), ((), ()))
    diag_part = lax.dot_general(
        panel_cols, panel_cols, contract_rows, preferred_element_type=jnp.float32
    )
    partial_value = lax.dot_general(
        flat_green, panel_cols, contract_rows, preferred_element_type=jnp.float32
    )
    diag_block = lax.psum(diag_part, "col")
    diag_block, partial_value = lax.optimization_barrier((diag_block, partial_value))
    normal_rows = lax.psum(partial_value, "col")

    far_holds = np.zeros((row_count, col_count), dtype=bool)
    for slot_no in range(far_slots):
        for c in range(col_count):
            far_holds[panel_tiles + slot_no * col_count + c, c] = True
    far_shared = tree_share(
        normal_rows[:tile_width], far_holds, ((32,), (1, 2)), (4, 8, 16), row_count, col_count
    )
    far_normal = jnp.roll(far_shared, -1, axis=0).reshape(far_slots * tile_width, PANEL)

    factor = jnp.linalg.cholesky(diag_block + jnp.diag(damping))
    factor_inv = lax.linalg.triangular_solve(
        factor, jnp.eye(PANEL, dtype=jnp.float32), left_side=True, lower=True
    )
    by_inverse = (((1,), (1,)), ((), ()))
    solved = lax.dot_general(
        normal_rows, factor_inv, by_inverse,
        precision=lax.Precision.HIGHEST, preferred_element_type=jnp.float32,
    )
    far_rows = lax.dot_general(
        far_normal, factor_inv, by_inverse,
        precision=lax.Precision.HIGHEST, preferred_element_type=jnp.float32,
    )
    solved = solved.reshape(tile_rows, tile_width, PANEL)
    tiles_list = []
    for local_no in range(tile_rows):
        tile_id = local_no * row_count + row_pos
        diag_rows = lax.dynamic_slice_in_dim(
            factor, jnp.minimum(tile_id, panel_tiles - 1) * tile_width, tile_width, 0
        )
        tiles_list.append(jnp.where(tile_id < panel_tiles, diag_rows, solved[local_no]))
    lower_rows = jnp.stack(tiles_list)
    col_share = PANEL // col_count
    chol_out = lax.dynamic_slice_in_dim(lower_rows, col_pos * col_share, col_share, 2)

    update = lax.dot_general(
        lower_rows.reshape(tile_rows * tile_width, PANEL),
        far_rows,
        (((1,), (1,)), ((), ())),
        precision=lax.Precision.HIGHEST,
        preferred_element_type=jnp.float32,
    )
    update = update.reshape(tile_rows, tile_width, far_slots, tile_width)
    tile_ids = jnp.arange(tile_rows, dtype=jnp.int32) * row_count + row_pos
    below_panel = (tile_ids >= panel_tiles)[:, None, None, None]
    return (chol_out, trail - jnp.where(below_panel, update, jnp.zeros_like(update)))


def solution(mesh):
    return jax.shard_map(
        local,
        mesh=mesh,
        in_specs=(
            P("col", None, "row"),
            P(None, None, "row"),
            P("col"),
            P("col"),
            P(),
            P(None, "row", None, "col"),
        ),
        out_specs=(P(None, "row", "col"), P(None, "row", None, "col")),
        check_vma=False,
    )
```

```python
import numpy as np
import jax
import jax.numpy as jnp
from jax import lax
from jax.sharding import PartitionSpec as P

NB = 128
PANEL = 512


def span_of(masks):
    values = [0]
    for mask in masks:
        values = values + [v ^ mask for v in values]
    return values


def spread_share(piece, holds, spread_rounds, row_count, col_count):
    row_pos = lax.axis_index("row")
    col_pos = lax.axis_index("col")
    flat_pos = row_pos * col_count + col_pos
    have = np.array(holds, dtype=bool)
    for round_masks in spread_rounds:
        gets_all = np.zeros_like(have)
        moved_list = []
        for mask in span_of(round_masks)[1:]:
            pairs = []
            gets = np.zeros_like(have)
            for r in range(row_count):
                for c in range(col_count):
                    if have[r, c] and not have[r ^ mask, c]:
                        pairs.append((r * col_count + c, (r ^ mask) * col_count + c))
                        gets[r ^ mask, c] = True
            assert not (gets & gets_all).any()
            gets_all = gets_all | gets
            moved_list.append((lax.ppermute(piece, ("row", "col"), pairs), gets))
        for moved, gets in moved_list:
            took = jnp.asarray(gets.reshape(-1))[flat_pos]
            piece = jnp.where(took, moved, piece)
        have = have | gets_all
    assert have.all()
    return piece


def gather_share(piece, gather_masks, row_count, col_count):
    row_pos = lax.axis_index("row")
    offsets = span_of(gather_masks)
    recv = [piece]
    for mask in offsets[1:]:
        pairs = [
            (r * col_count + c, (r ^ mask) * col_count + c)
            for r in range(row_count)
            for c in range(col_count)
        ]
        recv.append(lax.ppermute(piece, ("row", "col"), pairs))
    stacked = jnp.stack(recv)
    own_value = sum(
        jnp.where((row_pos & mask) != 0, 1 << bit, 0) for bit, mask in enumerate(gather_masks)
    )
    return jnp.stack(
        [lax.dynamic_index_in_dim(stacked, u ^ own_value, 0, keepdims=False) for u in range(len(offsets))]
    )


def local(green, arrival, row_gauge, row_time, damping, trail):
    row_count = lax.axis_size("row")
    col_count = lax.axis_size("col")
    row_pos = lax.axis_index("row")
    col_pos = lax.axis_index("col")
    kq_rows, tile_rows, tile_width = green.shape
    panel_tiles = PANEL // NB
    far_slots = trail.shape[2]
    arrive = arrival[row_gauge][:, :, 0]
    is_live = row_time[:, None] >= arrive
    masked = jnp.where(is_live[:, :, None], green, jnp.zeros_like(green))
    flat_green = masked.reshape(kq_rows, tile_rows * tile_width)

    panel_holds = np.zeros((row_count, col_count), dtype=bool)
    panel_holds[:panel_tiles, :] = True
    panel_piece = spread_share(
        masked[:, 0, :], panel_holds, ((8,), (32,), (4,), (16,)), row_count, col_count
    )
    panel_stack = gather_share(panel_piece, (1, 2), row_count, col_count)
    panel_cols = jnp.transpose(panel_stack, (1, 0, 2)).reshape(kq_rows, PANEL)

    contract_rows = (((0,), (0,)), ((), ()))
    diag_part = lax.dot_general(
        panel_cols, panel_cols, contract_rows, preferred_element_type=jnp.float32
    )
    partial_value = lax.dot_general(
        flat_green, panel_cols, contract_rows, preferred_element_type=jnp.float32
    )
    diag_block = lax.psum(diag_part, "col")
    diag_block, partial_value = lax.optimization_barrier((diag_block, partial_value))
    normal_rows = lax.psum(partial_value, "col")

    far_holds = np.zeros((row_count, col_count), dtype=bool)
    for slot_no in range(far_slots):
        for c in range(col_count):
            far_holds[panel_tiles + slot_no * col_count + c, c] = True
    far_piece = spread_share(
        normal_rows[:tile_width], far_holds, ((32,), (1, 2)), row_count, col_count
    )
    factor = jnp.linalg.cholesky(diag_block + jnp.diag(damping))
    factor, far_piece = lax.optimization_barrier((factor, far_piece))
    far_shared = gather_share(far_piece, (4, 8, 16), row_count, col_count)
    factor_inv = lax.linalg.triangular_solve(
        factor, jnp.eye(PANEL, dtype=jnp.float32), left_side=True, lower=True
    )
    factor_inv, far_shared = lax.optimization_barrier((factor_inv, far_shared))
    far_normal = jnp.roll(far_shared, -1, axis=0).reshape(far_slots * tile_width, PANEL)
    by_inverse = (((1,), (1,)), ((), ()))
    solved = lax.dot_general(
        normal_rows, factor_inv, by_inverse,
        precision=lax.Precision.HIGHEST, preferred_element_type=jnp.float32,
    )
    far_rows = lax.dot_general(
        far_normal, factor_inv, by_inverse,
        precision=lax.Precision.HIGHEST, preferred_element_type=jnp.float32,
    )
    solved = solved.reshape(tile_rows, tile_width, PANEL)
    tiles_list = []
    for local_no in range(tile_rows):
        tile_id = local_no * row_count + row_pos
        diag_rows = lax.dynamic_slice_in_dim(
            factor, jnp.minimum(tile_id, panel_tiles - 1) * tile_width, tile_width, 0
        )
        tiles_list.append(jnp.where(tile_id < panel_tiles, diag_rows, solved[local_no]))
    lower_rows = jnp.stack(tiles_list)
    col_share = PANEL // col_count
    chol_out = lax.dynamic_slice_in_dim(lower_rows, col_pos * col_share, col_share, 2)

    update = lax.dot_general(
        lower_rows.reshape(tile_rows * tile_width, PANEL),
        far_rows,
        (((1,), (1,)), ((), ())),
        precision=lax.Precision.HIGHEST,
        preferred_element_type=jnp.float32,
    )
    update = update.reshape(tile_rows, tile_width, far_slots, tile_width)
    tile_ids = jnp.arange(tile_rows, dtype=jnp.int32) * row_count + row_pos
    below_panel = (tile_ids >= panel_tiles)[:, None, None, None]
    return (chol_out, trail - jnp.where(below_panel, update, jnp.zeros_like(update)))


def solution(mesh):
    return jax.shard_map(
        local,
        mesh=mesh,
        in_specs=(
            P("col", None, "row"),
            P(None, None, "row"),
            P("col"),
            P("col"),
            P(),
            P(None, "row", None, "col"),
        ),
        out_specs=(P(None, "row", "col"), P(None, "row", None, "col")),
        check_vma=False,
    )
```

```python
import numpy as np
import jax
import jax.numpy as jnp
from jax import lax
from jax.sharding import PartitionSpec as P

NB = 128
PANEL = 512


def span_of(masks):
    values = [0]
    for mask in masks:
        values = values + [v ^ mask for v in values]
    return values


def spread_share(piece, holds, spread_rounds, row_count, col_count):
    row_pos = lax.axis_index("row")
    col_pos = lax.axis_index("col")
    flat_pos = row_pos * col_count + col_pos
    have = np.array(holds, dtype=bool)
    for round_masks in spread_rounds:
        gets_all = np.zeros_like(have)
        moved_list = []
        if isinstance(round_masks, list):
            mask_sets = [round_masks]
        else:
            mask_sets = [[mask, mask] for mask in span_of(round_masks)[1:]]
        for parity_masks in mask_sets:
            pairs = []
            gets = np.zeros_like(have)
            for r in range(row_count):
                mask = parity_masks[r % 2]
                for c in range(col_count):
                    if have[r, c] and not have[r ^ mask, c]:
                        pairs.append((r * col_count + c, (r ^ mask) * col_count + c))
                        gets[r ^ mask, c] = True
            assert not (gets & gets_all).any()
            gets_all = gets_all | gets
            moved_list.append((lax.ppermute(piece, ("row", "col"), pairs), gets))
        for moved, gets in moved_list:
            took = jnp.asarray(gets.reshape(-1))[flat_pos]
            piece = jnp.where(took, moved, piece)
        have = have | gets_all
    assert have.all()
    return piece


def gather_share(piece, gather_masks, row_count, col_count):
    row_pos = lax.axis_index("row")
    offsets = span_of(gather_masks)
    recv = [piece]
    for mask in offsets[1:]:
        pairs = [
            (r * col_count + c, (r ^ mask) * col_count + c)
            for r in range(row_count)
            for c in range(col_count)
        ]
        recv.append(lax.ppermute(piece, ("row", "col"), pairs))
    stacked = jnp.stack(recv)
    own_value = sum(
        jnp.where((row_pos & mask) != 0, 1 << bit, 0) for bit, mask in enumerate(gather_masks)
    )
    return jnp.stack(
        [lax.dynamic_index_in_dim(stacked, u ^ own_value, 0, keepdims=False) for u in range(len(offsets))]
    )


def local(green, arrival, row_gauge, row_time, damping, trail):
    row_count = lax.axis_size("row")
    col_count = lax.axis_size("col")
    row_pos = lax.axis_index("row")
    col_pos = lax.axis_index("col")
    kq_rows, tile_rows, tile_width = green.shape
    panel_tiles = PANEL // NB
    far_slots = trail.shape[2]
    arrive = arrival[row_gauge][:, :, 0]
    is_live = row_time[:, None] >= arrive
    masked = jnp.where(is_live[:, :, None], green, jnp.zeros_like(green))
    flat_green = masked.reshape(kq_rows, tile_rows * tile_width)

    panel_holds = np.zeros((row_count, col_count), dtype=bool)
    panel_holds[:panel_tiles, :] = True
    panel_piece = spread_share(
        masked[:, 0, :], panel_holds, [[8, 32], [32, 8], [4, 16], [16, 4]], row_count, col_count
    )
    panel_pair = gather_share(panel_piece, (2,), row_count, col_count)
    panel_stack = gather_share(panel_pair, (1,), row_count, col_count)
    panel_cols = jnp.transpose(panel_stack, (2, 1, 0, 3)).reshape(kq_rows, PANEL)

    contract_rows = (((0,), (0,)), ((), ()))
    half = PANEL // 2
    core_bit = row_pos % 2
    diag_part = lax.dot_general(
        lax.dynamic_slice_in_dim(panel_cols, core_bit * half, half, 1),
        panel_cols, contract_rows, preferred_element_type=jnp.float32,
    )
    partial_value = lax.dot_general(
        flat_green, panel_cols, contract_rows, preferred_element_type=jnp.float32
    )
    diag_half = lax.psum(diag_part, "col")
    swap_pairs = [
        (r * col_count + c, (r ^ 1) * col_count + c)
        for r in range(row_count)
        for c in range(col_count)
    ]
    other_half = lax.ppermute(diag_half, ("row", "col"), swap_pairs)
    diag_block = jnp.where(
        core_bit == 0,
        jnp.concatenate([diag_half, other_half]),
        jnp.concatenate([other_half, diag_half]),
    )
    diag_block, partial_value = lax.optimization_barrier((diag_block, partial_value))
    normal_rows = lax.psum(partial_value, "col")

    far_holds = np.zeros((row_count, col_count), dtype=bool)
    for slot_no in range(far_slots):
        for c in range(col_count):
            far_holds[panel_tiles + slot_no * col_count + c, c] = True
    far_piece = spread_share(
        normal_rows[:tile_width], far_holds, ((32,), (2,), (1,)), row_count, col_count
    )
    factor = jnp.linalg.cholesky(diag_block + jnp.diag(damping))
    factor, far_piece = lax.optimization_barrier((factor, far_piece))
    far_shared = gather_share(far_piece, (4, 8, 16), row_count, col_count)
    factor_inv = lax.linalg.triangular_solve(
        factor, jnp.eye(PANEL, dtype=jnp.float32), left_side=True, lower=True
    )
    factor_inv, far_shared = lax.optimization_barrier((factor_inv, far_shared))
    far_normal = jnp.roll(far_shared, -1, axis=0).reshape(far_slots * tile_width, PANEL)
    by_inverse = (((1,), (1,)), ((), ()))
    solved = lax.dot_general(
        normal_rows, factor_inv, by_inverse,
        precision=lax.Precision.HIGHEST, preferred_element_type=jnp.float32,
    )
    far_rows = lax.dot_general(
        far_normal, factor_inv, by_inverse,
        precision=lax.Precision.HIGHEST, preferred_element_type=jnp.float32,
    )
    solved = solved.reshape(tile_rows, tile_width, PANEL)
    tiles_list = []
    for local_no in range(tile_rows):
        tile_id = local_no * row_count + row_pos
        diag_rows = lax.dynamic_slice_in_dim(
            factor, jnp.minimum(tile_id, panel_tiles - 1) * tile_width, tile_width, 0
        )
        tiles_list.append(jnp.where(tile_id < panel_tiles, diag_rows, solved[local_no]))
    lower_rows = jnp.stack(tiles_list)
    col_share = PANEL // col_count
    chol_out = lax.dynamic_slice_in_dim(lower_rows, col_pos * col_share, col_share, 2)

    update = lax.dot_general(
        lower_rows.reshape(tile_rows * tile_width, PANEL),
        far_rows,
        (((1,), (1,)), ((), ())),
        precision=lax.Precision.HIGHEST,
        preferred_element_type=jnp.float32,
    )
    update = update.reshape(tile_rows, tile_width, far_slots, tile_width)
    tile_ids = jnp.arange(tile_rows, dtype=jnp.int32) * row_count + row_pos
    below_panel = (tile_ids >= panel_tiles)[:, None, None, None]
    return (chol_out, trail - jnp.where(below_panel, update, jnp.zeros_like(update)))


def solution(mesh):
    return jax.shard_map(
        local,
        mesh=mesh,
        in_specs=(
            P("col", None, "row"),
            P(None, None, "row"),
            P("col"),
            P("col"),
            P(),
            P(None, "row", None, "col"),
        ),
        out_specs=(P(None, "row", "col"), P(None, "row", None, "col")),
        check_vma=False,
    )
```

```python
import numpy as np
import jax
import jax.numpy as jnp
from jax import lax
from jax.sharding import PartitionSpec as P

NB = 128
PANEL = 512


def span_of(masks):
    values = [0]
    for mask in masks:
        values = values + [v ^ mask for v in values]
    return values


def spread_share(piece, holds, spread_rounds, row_count, col_count):
    row_pos = lax.axis_index("row")
    col_pos = lax.axis_index("col")
    flat_pos = row_pos * col_count + col_pos
    have = np.array(holds, dtype=bool)
    for round_masks in spread_rounds:
        gets_all = np.zeros_like(have)
        moved_list = []
        if isinstance(round_masks, list):
            mask_sets = [round_masks]
        else:
            mask_sets = [[mask, mask] for mask in span_of(round_masks)[1:]]
        for parity_masks in mask_sets:
            pairs = []
            gets = np.zeros_like(have)
            for r in range(row_count):
                mask = parity_masks[r % 2]
                for c in range(col_count):
                    if have[r, c] and not have[r ^ mask, c]:
                        pairs.append((r * col_count + c, (r ^ mask) * col_count + c))
                        gets[r ^ mask, c] = True
            assert not (gets & gets_all).any()
            gets_all = gets_all | gets
            moved_list.append((lax.ppermute(piece, ("row", "col"), pairs), gets))
        for moved, gets in moved_list:
            took = jnp.asarray(gets.reshape(-1))[flat_pos]
            piece = jnp.where(took, moved, piece)
        have = have | gets_all
    assert have.all()
    return piece


def gather_share(piece, gather_masks, row_count, col_count):
    row_pos = lax.axis_index("row")
    offsets = span_of(gather_masks)
    recv = [piece]
    for mask in offsets[1:]:
        pairs = [
            (r * col_count + c, (r ^ mask) * col_count + c)
            for r in range(row_count)
            for c in range(col_count)
        ]
        recv.append(lax.ppermute(piece, ("row", "col"), pairs))
    stacked = jnp.stack(recv)
    own_value = sum(
        jnp.where((row_pos & mask) != 0, 1 << bit, 0) for bit, mask in enumerate(gather_masks)
    )
    return jnp.stack(
        [lax.dynamic_index_in_dim(stacked, u ^ own_value, 0, keepdims=False) for u in range(len(offsets))]
    )


def local(green, arrival, row_gauge, row_time, damping, trail):
    row_count = lax.axis_size("row")
    col_count = lax.axis_size("col")
    row_pos = lax.axis_index("row")
    col_pos = lax.axis_index("col")
    kq_rows, tile_rows, tile_width = green.shape
    panel_tiles = PANEL // NB
    far_slots = trail.shape[2]
    arrive = arrival[row_gauge][:, :, 0]
    is_live = row_time[:, None] >= arrive
    masked = jnp.where(is_live[:, :, None], green, jnp.zeros_like(green))
    flat_green = masked.reshape(kq_rows, tile_rows * tile_width)

    panel_holds = np.zeros((row_count, col_count), dtype=bool)
    panel_holds[:panel_tiles, :] = True
    panel_piece = spread_share(
        masked[:, 0, :], panel_holds, [[8, 32], [32, 8], [4, 16], [16, 4]], row_count, col_count
    )
    panel_pair = gather_share(panel_piece, (2,), row_count, col_count)
    panel_stack = gather_share(panel_pair, (1,), row_count, col_count)
    panel_cols = jnp.transpose(panel_stack, (2, 1, 0, 3)).reshape(kq_rows, PANEL)

    contract_rows = (((0,), (0,)), ((), ()))
    half = PANEL // 2
    core_bit = row_pos % 2
    diag_part = lax.dot_general(
        lax.dynamic_slice_in_dim(panel_cols, core_bit * half, half, 1),
        panel_cols, contract_rows, preferred_element_type=jnp.float32,
    )
    partial_value = lax.dot_general(
        flat_green, panel_cols, contract_rows, preferred_element_type=jnp.float32
    )
    diag_half = diag_part
    col_mask = 1
    while col_mask < col_count:
        col_pairs = [
            (r * col_count + c, r * col_count + (c ^ col_mask))
            for r in range(row_count)
            for c in range(col_count)
        ]
        diag_half = diag_half + lax.ppermute(diag_half, ("row", "col"), col_pairs)
        col_mask *= 2
    swap_pairs = [
        (r * col_count + c, (r ^ 1) * col_count + c)
        for r in range(row_count)
        for c in range(col_count)
    ]
    other_half = lax.ppermute(diag_half, ("row", "col"), swap_pairs)
    diag_block = jnp.where(
        core_bit == 0,
        jnp.concatenate([diag_half, other_half]),
        jnp.concatenate([other_half, diag_half]),
    )
    diag_block, partial_value = lax.optimization_barrier((diag_block, partial_value))
    normal_rows = lax.psum(partial_value, "col")

    far_holds = np.zeros((row_count, col_count), dtype=bool)
    for slot_no in range(far_slots):
        for c in range(col_count):
            far_holds[panel_tiles + slot_no * col_count + c, c] = True
    far_piece = spread_share(
        normal_rows[:tile_width], far_holds, ((32,), (2,), (1,)), row_count, col_count
    )
    factor = jnp.linalg.cholesky(diag_block + jnp.diag(damping))
    factor, far_piece = lax.optimization_barrier((factor, far_piece))
    far_shared = gather_share(far_piece, (4, 8, 16), row_count, col_count)
    factor_inv = lax.linalg.triangular_solve(
        factor, jnp.eye(PANEL, dtype=jnp.float32), left_side=True, lower=True
    )
    factor_inv, far_shared = lax.optimization_barrier((factor_inv, far_shared))
    far_normal = jnp.roll(far_shared, -1, axis=0).reshape(far_slots * tile_width, PANEL)
    by_inverse = (((1,), (1,)), ((), ()))
    solved = lax.dot_general(
        normal_rows, factor_inv, by_inverse,
        precision=lax.Precision.HIGHEST, preferred_element_type=jnp.float32,
    )
    far_rows = lax.dot_general(
        far_normal, factor_inv, by_inverse,
        precision=lax.Precision.HIGHEST, preferred_element_type=jnp.float32,
    )
    solved = solved.reshape(tile_rows, tile_width, PANEL)
    tiles_list = []
    for local_no in range(tile_rows):
        tile_id = local_no * row_count + row_pos
        diag_rows = lax.dynamic_slice_in_dim(
            factor, jnp.minimum(tile_id, panel_tiles - 1) * tile_width, tile_width, 0
        )
        tiles_list.append(jnp.where(tile_id < panel_tiles, diag_rows, solved[local_no]))
    lower_rows = jnp.stack(tiles_list)
    col_share = PANEL // col_count
    chol_out = lax.dynamic_slice_in_dim(lower_rows, col_pos * col_share, col_share, 2)

    update = lax.dot_general(
        lower_rows.reshape(tile_rows * tile_width, PANEL),
        far_rows,
        (((1,), (1,)), ((), ())),
        precision=lax.Precision.HIGHEST,
        preferred_element_type=jnp.float32,
    )
    update = update.reshape(tile_rows, tile_width, far_slots, tile_width)
    tile_ids = jnp.arange(tile_rows, dtype=jnp.int32) * row_count + row_pos
    below_panel = (tile_ids >= panel_tiles)[:, None, None, None]
    return (chol_out, trail - jnp.where(below_panel, update, jnp.zeros_like(update)))


def solution(mesh):
    return jax.shard_map(
        local,
        mesh=mesh,
        in_specs=(
            P("col", None, "row"),
            P(None, None, "row"),
            P("col"),
            P("col"),
            P(),
            P(None, "row", None, "col"),
        ),
        out_specs=(P(None, "row", "col"), P(None, "row", None, "col")),
        check_vma=False,
    )
```

```python
import numpy as np
import jax
import jax.numpy as jnp
from jax import lax
from jax.sharding import PartitionSpec as P

NB = 128
PANEL = 512


def span_of(masks):
    values = [0]
    for mask in masks:
        values = values + [v ^ mask for v in values]
    return values


def spread_share(piece, holds, spread_rounds, row_count, col_count):
    row_pos = lax.axis_index("row")
    col_pos = lax.axis_index("col")
    flat_pos = row_pos * col_count + col_pos
    have = np.array(holds, dtype=bool)
    for round_masks in spread_rounds:
        gets_all = np.zeros_like(have)
        moved_list = []
        if isinstance(round_masks, list):
            mask_sets = [round_masks]
        else:
            mask_sets = [[mask, mask] for mask in span_of(round_masks)[1:]]
        for parity_masks in mask_sets:
            pairs = []
            gets = np.zeros_like(have)
            for r in range(row_count):
                mask = parity_masks[r % 2]
                for c in range(col_count):
                    if have[r, c] and not have[r ^ mask, c]:
                        pairs.append((r * col_count + c, (r ^ mask) * col_count + c))
                        gets[r ^ mask, c] = True
            assert not (gets & gets_all).any()
            gets_all = gets_all | gets
            moved_list.append((lax.ppermute(piece, ("row", "col"), pairs), gets))
        for moved, gets in moved_list:
            took = jnp.asarray(gets.reshape(-1))[flat_pos]
            piece = jnp.where(took, moved, piece)
        have = have | gets_all
    assert have.all()
    return piece


def gather_share(piece, gather_masks, row_count, col_count):
    row_pos = lax.axis_index("row")
    offsets = span_of(gather_masks)
    recv = [piece]
    for mask in offsets[1:]:
        pairs = [
            (r * col_count + c, (r ^ mask) * col_count + c)
            for r in range(row_count)
            for c in range(col_count)
        ]
        recv.append(lax.ppermute(piece, ("row", "col"), pairs))
    stacked = jnp.stack(recv)
    own_value = sum(
        jnp.where((row_pos & mask) != 0, 1 << bit, 0) for bit, mask in enumerate(gather_masks)
    )
    return jnp.stack(
        [lax.dynamic_index_in_dim(stacked, u ^ own_value, 0, keepdims=False) for u in range(len(offsets))]
    )


def lower_inverse_from_blocks(factor, inv_diag, nb):
    inv = jnp.stack(inv_diag)
    size = nb
    while inv.shape[0] > 1:
        pair_count = inv.shape[0] // 2
        first_inv = inv[0::2]
        second_inv = inv[1::2]
        below = jnp.stack([
            factor[(2 * p + 1) * size:(2 * p + 2) * size, 2 * p * size:(2 * p + 1) * size]
            for p in range(pair_count)
        ])
        low = -jnp.einsum("pij,pjk,pkl->pil", second_inv, below, first_inv, precision=lax.Precision.HIGHEST)
        top = jnp.concatenate([first_inv, jnp.zeros_like(first_inv)], axis=2)
        bottom = jnp.concatenate([low, second_inv], axis=2)
        inv = jnp.concatenate([top, bottom], axis=1)
        size *= 2
    return inv[0]


def local(green, arrival, row_gauge, row_time, damping, trail):
    row_count = lax.axis_size("row")
    col_count = lax.axis_size("col")
    row_pos = lax.axis_index("row")
    col_pos = lax.axis_index("col")
    kq_rows, tile_rows, tile_width = green.shape
    panel_tiles = PANEL // NB
    far_slots = trail.shape[2]
    arrive = arrival[row_gauge][:, :, 0]
    is_live = row_time[:, None] >= arrive
    masked = jnp.where(is_live[:, :, None], green, jnp.zeros_like(green))
    flat_green = masked.reshape(kq_rows, tile_rows * tile_width)

    panel_holds = np.zeros((row_count, col_count), dtype=bool)
    panel_holds[:panel_tiles, :] = True
    panel_piece = spread_share(
        masked[:, 0, :], panel_holds, [[8, 32], [32, 8], [4, 16], [16, 4]], row_count, col_count
    )
    panel_pair = gather_share(panel_piece, (2,), row_count, col_count)
    panel_stack = gather_share(panel_pair, (1,), row_count, col_count)
    panel_cols = jnp.transpose(panel_stack, (2, 1, 0, 3)).reshape(kq_rows, PANEL)

    contract_rows = (((0,), (0,)), ((), ()))
    half = PANEL // 2
    core_bit = row_pos % 2
    diag_part = lax.dot_general(
        lax.dynamic_slice_in_dim(panel_cols, core_bit * half, half, 1),
        panel_cols, contract_rows, preferred_element_type=jnp.float32,
    )
    partial_value = lax.dot_general(
        flat_green, panel_cols, contract_rows, preferred_element_type=jnp.float32
    )
    diag_half = diag_part
    col_mask = 1
    while col_mask < col_count:
        col_pairs = [
            (r * col_count + c, r * col_count + (c ^ col_mask))
            for r in range(row_count)
            for c in range(col_count)
        ]
        diag_half = diag_half + lax.ppermute(diag_half, ("row", "col"), col_pairs)
        col_mask *= 2
    swap_pairs = [
        (r * col_count + c, (r ^ 1) * col_count + c)
        for r in range(row_count)
        for c in range(col_count)
    ]
    other_half = lax.ppermute(diag_half, ("row", "col"), swap_pairs)
    diag_block = jnp.where(
        core_bit == 0,
        jnp.concatenate([diag_half, other_half]),
        jnp.concatenate([other_half, diag_half]),
    )
    diag_block, partial_value = lax.optimization_barrier((diag_block, partial_value))
    normal_rows = lax.psum(partial_value, "col")

    far_holds = np.zeros((row_count, col_count), dtype=bool)
    for slot_no in range(far_slots):
        for c in range(col_count):
            far_holds[panel_tiles + slot_no * col_count + c, c] = True
    far_piece = spread_share(
        normal_rows[:tile_width], far_holds, ((32,), (2,), (1,)), row_count, col_count
    )
    by_inverse = (((1,), (1,)), ((), ()))
    unit = jnp.eye(tile_width, dtype=jnp.float32)
    trailing = diag_block + jnp.diag(damping)
    factor_cols = []
    inv_diag = []
    for step in range(panel_tiles):
        head = trailing[:tile_width, :tile_width]
        head_factor = jnp.tril(jnp.linalg.cholesky(head))
        head_inv = lax.linalg.triangular_solve(head_factor, unit, left_side=True, lower=True)
        inv_diag.append(head_inv)
        if step + 1 < panel_tiles:
            panel = lax.dot_general(
                trailing[tile_width:, :tile_width], head_inv, by_inverse,
                precision=lax.Precision.HIGHEST, preferred_element_type=jnp.float32,
            )
            trailing = trailing[tile_width:, tile_width:] - lax.dot_general(
                panel, panel, by_inverse,
                precision=lax.Precision.HIGHEST, preferred_element_type=jnp.float32,
            )
            factor_cols.append(jnp.concatenate([head_factor, panel]))
        else:
            factor_cols.append(head_factor)
        if step == 1:
            trailing, far_piece = lax.optimization_barrier((trailing, far_piece))
    factor = jnp.concatenate(
        [jnp.pad(col, ((step * tile_width, 0), (0, 0))) for step, col in enumerate(factor_cols)],
        axis=1,
    )
    far_shared = gather_share(far_piece, (4, 8, 16), row_count, col_count)
    factor_inv = lower_inverse_from_blocks(factor, inv_diag, tile_width)
    factor_inv, far_shared = lax.optimization_barrier((factor_inv, far_shared))
    far_normal = jnp.roll(far_shared, -1, axis=0).reshape(far_slots * tile_width, PANEL)
    solved = lax.dot_general(
        normal_rows, factor_inv, by_inverse,
        precision=lax.Precision.HIGHEST, preferred_element_type=jnp.float32,
    )
    far_rows = lax.dot_general(
        far_normal, factor_inv, by_inverse,
        precision=lax.Precision.HIGHEST, preferred_element_type=jnp.float32,
    )
    solved = solved.reshape(tile_rows, tile_width, PANEL)
    tiles_list = []
    for local_no in range(tile_rows):
        tile_id = local_no * row_count + row_pos
        diag_rows = lax.dynamic_slice_in_dim(
            factor, jnp.minimum(tile_id, panel_tiles - 1) * tile_width, tile_width, 0
        )
        tiles_list.append(jnp.where(tile_id < panel_tiles, diag_rows, solved[local_no]))
    lower_rows = jnp.stack(tiles_list)
    col_share = PANEL // col_count
    chol_out = lax.dynamic_slice_in_dim(lower_rows, col_pos * col_share, col_share, 2)

    update = lax.dot_general(
        lower_rows.reshape(tile_rows * tile_width, PANEL),
        far_rows,
        (((1,), (1,)), ((), ())),
        precision=lax.Precision.HIGHEST,
        preferred_element_type=jnp.float32,
    )
    update = update.reshape(tile_rows, tile_width, far_slots, tile_width)
    tile_ids = jnp.arange(tile_rows, dtype=jnp.int32) * row_count + row_pos
    below_panel = (tile_ids >= panel_tiles)[:, None, None, None]
    return (chol_out, trail - jnp.where(below_panel, update, jnp.zeros_like(update)))


def solution(mesh):
    return jax.shard_map(
        local,
        mesh=mesh,
        in_specs=(
            P("col", None, "row"),
            P(None, None, "row"),
            P("col"),
            P("col"),
            P(),
            P(None, "row", None, "col"),
        ),
        out_specs=(P(None, "row", "col"), P(None, "row", None, "col")),
        check_vma=False,
    )
```

```python
import numpy as np
import jax
import jax.numpy as jnp
from jax import lax
from jax.sharding import PartitionSpec as P

NB = 128
PANEL = 512


def span_of(masks):
    values = [0]
    for mask in masks:
        values = values + [v ^ mask for v in values]
    return values


def spread_share(piece, holds, spread_rounds, row_count, col_count):
    row_pos = lax.axis_index("row")
    col_pos = lax.axis_index("col")
    flat_pos = row_pos * col_count + col_pos
    have = np.array(holds, dtype=bool)
    for round_masks in spread_rounds:
        gets_all = np.zeros_like(have)
        moved_list = []
        if isinstance(round_masks, list):
            mask_sets = [round_masks]
        else:
            mask_sets = [[mask, mask] for mask in span_of(round_masks)[1:]]
        for parity_masks in mask_sets:
            pairs = []
            gets = np.zeros_like(have)
            for r in range(row_count):
                mask = parity_masks[r % 2]
                for c in range(col_count):
                    if have[r, c] and not have[r ^ mask, c]:
                        pairs.append((r * col_count + c, (r ^ mask) * col_count + c))
                        gets[r ^ mask, c] = True
            assert not (gets & gets_all).any()
            gets_all = gets_all | gets
            moved_list.append((lax.ppermute(piece, ("row", "col"), pairs), gets))
        for moved, gets in moved_list:
            took = jnp.asarray(gets.reshape(-1))[flat_pos]
            piece = jnp.where(took, moved, piece)
        have = have | gets_all
    assert have.all()
    return piece


def gather_share(piece, gather_masks, row_count, col_count):
    row_pos = lax.axis_index("row")
    offsets = span_of(gather_masks)
    recv = [piece]
    for mask in offsets[1:]:
        pairs = [
            (r * col_count + c, (r ^ mask) * col_count + c)
            for r in range(row_count)
            for c in range(col_count)
        ]
        recv.append(lax.ppermute(piece, ("row", "col"), pairs))
    stacked = jnp.stack(recv)
    own_value = sum(
        jnp.where((row_pos & mask) != 0, 1 << bit, 0) for bit, mask in enumerate(gather_masks)
    )
    return jnp.stack(
        [lax.dynamic_index_in_dim(stacked, u ^ own_value, 0, keepdims=False) for u in range(len(offsets))]
    )


def lower_inverse_from_blocks(factor, inv_diag, nb):
    inv = jnp.stack(inv_diag)
    size = nb
    while inv.shape[0] > 1:
        pair_count = inv.shape[0] // 2
        first_inv = inv[0::2]
        second_inv = inv[1::2]
        below = jnp.stack([
            factor[(2 * p + 1) * size:(2 * p + 2) * size, 2 * p * size:(2 * p + 1) * size]
            for p in range(pair_count)
        ])
        low = -jnp.einsum("pij,pjk,pkl->pil", second_inv, below, first_inv, precision=lax.Precision.HIGHEST)
        top = jnp.concatenate([first_inv, jnp.zeros_like(first_inv)], axis=2)
        bottom = jnp.concatenate([low, second_inv], axis=2)
        inv = jnp.concatenate([top, bottom], axis=1)
        size *= 2
    return inv[0]


def local(green, arrival, row_gauge, row_time, damping, trail):
    row_count = lax.axis_size("row")
    col_count = lax.axis_size("col")
    row_pos = lax.axis_index("row")
    col_pos = lax.axis_index("col")
    kq_rows, tile_rows, tile_width = green.shape
    panel_tiles = PANEL // NB
    far_slots = trail.shape[2]
    arrive = arrival[row_gauge][:, :, 0]
    is_live = row_time[:, None] >= arrive
    masked = jnp.where(is_live[:, :, None], green, jnp.zeros_like(green))
    flat_green = masked.reshape(kq_rows, tile_rows * tile_width)

    panel_holds = np.zeros((row_count, col_count), dtype=bool)
    panel_holds[:panel_tiles, :] = True
    panel_piece = spread_share(
        masked[:, 0, :], panel_holds, [[8, 32], [32, 8], [4, 16], [16, 4]], row_count, col_count
    )
    panel_pair = gather_share(panel_piece, (2,), row_count, col_count)
    panel_stack = gather_share(panel_pair, (1,), row_count, col_count)
    panel_cols = jnp.transpose(panel_stack, (2, 1, 0, 3)).reshape(kq_rows, PANEL)

    contract_rows = (((0,), (0,)), ((), ()))
    half = PANEL // 2
    core_bit = row_pos % 2
    diag_part = lax.dot_general(
        lax.dynamic_slice_in_dim(panel_cols, core_bit * half, half, 1),
        panel_cols, contract_rows, preferred_element_type=jnp.float32,
    )
    partial_value = lax.dot_general(
        flat_green, panel_cols, contract_rows, preferred_element_type=jnp.float32
    )
    diag_half = diag_part
    col_mask = 1
    while col_mask < col_count:
        col_pairs = [
            (r * col_count + c, r * col_count + (c ^ col_mask))
            for r in range(row_count)
            for c in range(col_count)
        ]
        diag_half = diag_half + lax.ppermute(diag_half, ("row", "col"), col_pairs)
        col_mask *= 2
    swap_pairs = [
        (r * col_count + c, (r ^ 1) * col_count + c)
        for r in range(row_count)
        for c in range(col_count)
    ]
    other_half = lax.ppermute(diag_half, ("row", "col"), swap_pairs)
    diag_block = jnp.where(
        core_bit == 0,
        jnp.concatenate([diag_half, other_half]),
        jnp.concatenate([other_half, diag_half]),
    )
    head_rows = partial_value[:tile_width]
    col_mask = 1
    while col_mask < col_count:
        col_pairs = [
            (r * col_count + c, r * col_count + (c ^ col_mask))
            for r in range(row_count)
            for c in range(col_count)
        ]
        head_rows = head_rows + lax.ppermute(head_rows, ("row", "col"), col_pairs)
        col_mask *= 2
    diag_block, rest_rows = lax.optimization_barrier((diag_block, partial_value[tile_width:]))
    normal_rows = jnp.concatenate([head_rows, lax.psum(rest_rows, "col")])

    far_holds = np.zeros((row_count, col_count), dtype=bool)
    for slot_no in range(far_slots):
        for c in range(col_count):
            far_holds[panel_tiles + slot_no * col_count + c, c] = True
    far_piece = spread_share(
        head_rows, far_holds, ((32,), (2,), (1,)), row_count, col_count
    )
    by_inverse = (((1,), (1,)), ((), ()))
    unit = jnp.eye(tile_width, dtype=jnp.float32)
    trailing = diag_block + jnp.diag(damping)
    factor_cols = []
    inv_diag = []
    for step in range(panel_tiles):
        head = trailing[:tile_width, :tile_width]
        head_factor = jnp.tril(jnp.linalg.cholesky(head))
        head_inv = lax.linalg.triangular_solve(head_factor, unit, left_side=True, lower=True)
        inv_diag.append(head_inv)
        if step + 1 < panel_tiles:
            panel = lax.dot_general(
                trailing[tile_width:, :tile_width], head_inv, by_inverse,
                precision=lax.Precision.HIGHEST, preferred_element_type=jnp.float32,
            )
            trailing = trailing[tile_width:, tile_width:] - lax.dot_general(
                panel, panel, by_inverse,
                precision=lax.Precision.HIGHEST, preferred_element_type=jnp.float32,
            )
            factor_cols.append(jnp.concatenate([head_factor, panel]))
        else:
            factor_cols.append(head_factor)
        if step == 0:
            trailing, far_piece = lax.optimization_barrier((trailing, far_piece))
            far_shared = gather_share(far_piece, (4, 8, 16), row_count, col_count)
        if step == 2:
            trailing, far_shared = lax.optimization_barrier((trailing, far_shared))
    factor = jnp.concatenate(
        [jnp.pad(col, ((step * tile_width, 0), (0, 0))) for step, col in enumerate(factor_cols)],
        axis=1,
    )
    factor_inv = lower_inverse_from_blocks(factor, inv_diag, tile_width)
    far_normal = jnp.roll(far_shared, -1, axis=0).reshape(far_slots * tile_width, PANEL)
    solved = lax.dot_general(
        normal_rows, factor_inv, by_inverse,
        precision=lax.Precision.HIGHEST, preferred_element_type=jnp.float32,
    )
    far_rows = lax.dot_general(
        far_normal, factor_inv, by_inverse,
        precision=lax.Precision.HIGHEST, preferred_element_type=jnp.float32,
    )
    solved = solved.reshape(tile_rows, tile_width, PANEL)
    tiles_list = []
    for local_no in range(tile_rows):
        tile_id = local_no * row_count + row_pos
        diag_rows = lax.dynamic_slice_in_dim(
            factor, jnp.minimum(tile_id, panel_tiles - 1) * tile_width, tile_width, 0
        )
        tiles_list.append(jnp.where(tile_id < panel_tiles, diag_rows, solved[local_no]))
    lower_rows = jnp.stack(tiles_list)
    col_share = PANEL // col_count
    chol_out = lax.dynamic_slice_in_dim(lower_rows, col_pos * col_share, col_share, 2)

    update = lax.dot_general(
        lower_rows.reshape(tile_rows * tile_width, PANEL),
        far_rows,
        (((1,), (1,)), ((), ())),
        precision=lax.Precision.HIGHEST,
        preferred_element_type=jnp.float32,
    )
    update = update.reshape(tile_rows, tile_width, far_slots, tile_width)
    tile_ids = jnp.arange(tile_rows, dtype=jnp.int32) * row_count + row_pos
    below_panel = (tile_ids >= panel_tiles)[:, None, None, None]
    return (chol_out, trail - jnp.where(below_panel, update, jnp.zeros_like(update)))


def solution(mesh):
    return jax.shard_map(
        local,
        mesh=mesh,
        in_specs=(
            P("col", None, "row"),
            P(None, None, "row"),
            P("col"),
            P("col"),
            P(),
            P(None, "row", None, "col"),
        ),
        out_specs=(P(None, "row", "col"), P(None, "row", None, "col")),
        check_vma=False,
    )
```

```python
import numpy as np
import jax
import jax.numpy as jnp
from jax import lax
from jax.sharding import PartitionSpec as P

NB = 128
PANEL = 512


def span_of(masks):
    values = [0]
    for mask in masks:
        values = values + [v ^ mask for v in values]
    return values


def spread_share(piece, holds, spread_rounds, row_count, col_count):
    row_pos = lax.axis_index("row")
    col_pos = lax.axis_index("col")
    flat_pos = row_pos * col_count + col_pos
    have = np.array(holds, dtype=bool)
    for round_masks in spread_rounds:
        gets_all = np.zeros_like(have)
        moved_list = []
        if isinstance(round_masks, list):
            mask_sets = [round_masks]
        else:
            mask_sets = [[mask, mask] for mask in span_of(round_masks)[1:]]
        for parity_masks in mask_sets:
            pairs = []
            gets = np.zeros_like(have)
            for r in range(row_count):
                mask = parity_masks[r % 2]
                for c in range(col_count):
                    if have[r, c] and not have[r ^ mask, c]:
                        pairs.append((r * col_count + c, (r ^ mask) * col_count + c))
                        gets[r ^ mask, c] = True
            assert not (gets & gets_all).any()
            gets_all = gets_all | gets
            moved_list.append((lax.ppermute(piece, ("row", "col"), pairs), gets))
        for moved, gets in moved_list:
            took = jnp.asarray(gets.reshape(-1))[flat_pos]
            piece = jnp.where(took, moved, piece)
        have = have | gets_all
    assert have.all()
    return piece


def gather_share(piece, gather_masks, row_count, col_count):
    row_pos = lax.axis_index("row")
    offsets = span_of(gather_masks)
    recv = [piece]
    for mask in offsets[1:]:
        pairs = [
            (r * col_count + c, (r ^ mask) * col_count + c)
            for r in range(row_count)
            for c in range(col_count)
        ]
        recv.append(lax.ppermute(piece, ("row", "col"), pairs))
    stacked = jnp.stack(recv)
    own_value = sum(
        jnp.where((row_pos & mask) != 0, 1 << bit, 0) for bit, mask in enumerate(gather_masks)
    )
    return jnp.stack(
        [lax.dynamic_index_in_dim(stacked, u ^ own_value, 0, keepdims=False) for u in range(len(offsets))]
    )


def lower_inverse_from_blocks(factor, inv_diag, nb):
    inv = jnp.stack(inv_diag)
    size = nb
    while inv.shape[0] > 1:
        pair_count = inv.shape[0] // 2
        first_inv = inv[0::2]
        second_inv = inv[1::2]
        below = jnp.stack([
            factor[(2 * p + 1) * size:(2 * p + 2) * size, 2 * p * size:(2 * p + 1) * size]
            for p in range(pair_count)
        ])
        low = -jnp.einsum("pij,pjk,pkl->pil", second_inv, below, first_inv, precision=lax.Precision.HIGHEST)
        top = jnp.concatenate([first_inv, jnp.zeros_like(first_inv)], axis=2)
        bottom = jnp.concatenate([low, second_inv], axis=2)
        inv = jnp.concatenate([top, bottom], axis=1)
        size *= 2
    return inv[0]


def local(green, arrival, row_gauge, row_time, damping, trail):
    row_count = lax.axis_size("row")
    col_count = lax.axis_size("col")
    row_pos = lax.axis_index("row")
    col_pos = lax.axis_index("col")
    kq_rows, tile_rows, tile_width = green.shape
    panel_tiles = PANEL // NB
    far_slots = trail.shape[2]
    arrive = arrival[row_gauge][:, :, 0]
    is_live = row_time[:, None] >= arrive
    masked = jnp.where(is_live[:, :, None], green, jnp.zeros_like(green))
    flat_green = masked.reshape(kq_rows, tile_rows * tile_width)

    panel_holds = np.zeros((row_count, col_count), dtype=bool)
    panel_holds[:panel_tiles, :] = True
    panel_piece = spread_share(
        masked[:, 0, :], panel_holds, [[8, 32], [32, 8], [4, 16], [16, 4]], row_count, col_count
    )
    panel_pair = gather_share(panel_piece, (2,), row_count, col_count)
    panel_stack = gather_share(panel_pair, (1,), row_count, col_count)
    panel_cols = jnp.transpose(panel_stack, (2, 1, 0, 3)).reshape(kq_rows, PANEL)

    contract_rows = (((0,), (0,)), ((), ()))
    half = PANEL // 2
    core_bit = row_pos % 2
    diag_part = lax.dot_general(
        lax.dynamic_slice_in_dim(panel_cols, core_bit * half, half, 1),
        panel_cols, contract_rows, preferred_element_type=jnp.float32,
    )
    partial_value = lax.dot_general(
        flat_green, panel_cols, contract_rows, preferred_element_type=jnp.float32
    )
    diag_half = diag_part
    col_mask = 1
    while col_mask < col_count:
        col_pairs = [
            (r * col_count + c, r * col_count + (c ^ col_mask))
            for r in range(row_count)
            for c in range(col_count)
        ]
        diag_half = diag_half + lax.ppermute(diag_half, ("row", "col"), col_pairs)
        col_mask *= 2
    swap_pairs = [
        (r * col_count + c, (r ^ 1) * col_count + c)
        for r in range(row_count)
        for c in range(col_count)
    ]
    other_half = lax.ppermute(diag_half, ("row", "col"), swap_pairs)
    diag_block = jnp.where(
        core_bit == 0,
        jnp.concatenate([diag_half, other_half]),
        jnp.concatenate([other_half, diag_half]),
    )
    head_rows = partial_value[:tile_width]
    col_mask = 1
    while col_mask < col_count:
        col_pairs = [
            (r * col_count + c, r * col_count + (c ^ col_mask))
            for r in range(row_count)
            for c in range(col_count)
        ]
        head_rows = head_rows + lax.ppermute(head_rows, ("row", "col"), col_pairs)
        col_mask *= 2
    diag_block, rest_rows = lax.optimization_barrier((diag_block, partial_value[tile_width:]))
    normal_rows = jnp.concatenate([head_rows, lax.psum(rest_rows, "col")])

    far_holds = np.zeros((row_count, col_count), dtype=bool)
    for slot_no in range(far_slots):
        for c in range(col_count):
            far_holds[panel_tiles + slot_no * col_count + c, c] = True
    far_piece = spread_share(
        head_rows, far_holds, ((32,), (2,), (1,)), row_count, col_count
    )
    by_inverse = (((1,), (1,)), ((), ()))
    unit = jnp.eye(tile_width, dtype=jnp.float32)
    trailing = diag_block + jnp.diag(damping)
    factor_cols = []
    inv_diag = []
    for step in range(panel_tiles):
        head = trailing[:tile_width, :tile_width]
        head_factor = jnp.tril(jnp.linalg.cholesky(head))
        head_inv = lax.linalg.triangular_solve(head_factor, unit, left_side=True, lower=True)
        inv_diag.append(head_inv)
        if step + 1 < panel_tiles:
            panel = lax.dot_general(
                trailing[tile_width:, :tile_width], head_inv, by_inverse,
                precision=lax.Precision.HIGHEST, preferred_element_type=jnp.float32,
            )
            trailing = trailing[tile_width:, tile_width:] - lax.dot_general(
                panel, panel, by_inverse,
                precision=lax.Precision.HIGHEST, preferred_element_type=jnp.float32,
            )
            factor_cols.append(jnp.concatenate([head_factor, panel]))
        else:
            factor_cols.append(head_factor)
        if step == 0:
            trailing, far_piece = lax.optimization_barrier((trailing, far_piece))
            far_shared = gather_share(far_piece, (4, 8, 16), row_count, col_count)
        if step == 2:
            trailing, far_shared = lax.optimization_barrier((trailing, far_shared))
    factor = jnp.concatenate(
        [jnp.pad(col, ((step * tile_width, 0), (0, 0))) for step, col in enumerate(factor_cols)],
        axis=1,
    )
    factor_inv = lower_inverse_from_blocks(factor, inv_diag, tile_width)
    far_normal = jnp.roll(far_shared, -1, axis=0).reshape(far_slots * tile_width, PANEL)
    solved = lax.dot_general(
        normal_rows, factor_inv, by_inverse,
        precision=lax.Precision.HIGH, preferred_element_type=jnp.float32,
    )
    far_rows = lax.dot_general(
        far_normal, factor_inv, by_inverse,
        precision=lax.Precision.HIGH, preferred_element_type=jnp.float32,
    )
    solved = solved.reshape(tile_rows, tile_width, PANEL)
    tiles_list = []
    for local_no in range(tile_rows):
        tile_id = local_no * row_count + row_pos
        diag_rows = lax.dynamic_slice_in_dim(
            factor, jnp.minimum(tile_id, panel_tiles - 1) * tile_width, tile_width, 0
        )
        tiles_list.append(jnp.where(tile_id < panel_tiles, diag_rows, solved[local_no]))
    lower_rows = jnp.stack(tiles_list)
    col_share = PANEL // col_count
    chol_out = lax.dynamic_slice_in_dim(lower_rows, col_pos * col_share, col_share, 2)

    update = lax.dot_general(
        lower_rows.reshape(tile_rows * tile_width, PANEL),
        far_rows,
        (((1,), (1,)), ((), ())),
        precision=lax.Precision.HIGH,
        preferred_element_type=jnp.float32,
    )
    update = update.reshape(tile_rows, tile_width, far_slots, tile_width)
    tile_ids = jnp.arange(tile_rows, dtype=jnp.int32) * row_count + row_pos
    below_panel = (tile_ids >= panel_tiles)[:, None, None, None]
    return (chol_out, trail - jnp.where(below_panel, update, jnp.zeros_like(update)))


def solution(mesh):
    return jax.shard_map(
        local,
        mesh=mesh,
        in_specs=(
            P("col", None, "row"),
            P(None, None, "row"),
            P("col"),
            P("col"),
            P(),
            P(None, "row", None, "col"),
        ),
        out_specs=(P(None, "row", "col"), P(None, "row", None, "col")),
        check_vma=False,
    )
```

```python
import numpy as np
import jax
import jax.numpy as jnp
from jax import lax
from jax.sharding import PartitionSpec as P

NB = 128
PANEL = 512


def span_of(masks):
    values = [0]
    for mask in masks:
        values = values + [v ^ mask for v in values]
    return values


def spread_share(piece, holds, spread_rounds, row_count, col_count):
    row_pos = lax.axis_index("row")
    col_pos = lax.axis_index("col")
    flat_pos = row_pos * col_count + col_pos
    have = np.array(holds, dtype=bool)
    for round_masks in spread_rounds:
        gets_all = np.zeros_like(have)
        moved_list = []
        if isinstance(round_masks, list):
            mask_sets = [round_masks]
        else:
            mask_sets = [[mask, mask] for mask in span_of(round_masks)[1:]]
        for parity_masks in mask_sets:
            pairs = []
            gets = np.zeros_like(have)
            for r in range(row_count):
                mask = parity_masks[r % 2]
                for c in range(col_count):
                    if have[r, c] and not have[r ^ mask, c]:
                        pairs.append((r * col_count + c, (r ^ mask) * col_count + c))
                        gets[r ^ mask, c] = True
            assert not (gets & gets_all).any()
            gets_all = gets_all | gets
            moved_list.append((lax.ppermute(piece, ("row", "col"), pairs), gets))
        for moved, gets in moved_list:
            took = jnp.asarray(gets.reshape(-1))[flat_pos]
            piece = jnp.where(took, moved, piece)
        have = have | gets_all
    assert have.all()
    return piece


def gather_share(piece, gather_masks, row_count, col_count):
    row_pos = lax.axis_index("row")
    offsets = span_of(gather_masks)
    recv = [piece]
    for mask in offsets[1:]:
        pairs = [
            (r * col_count + c, (r ^ mask) * col_count + c)
            for r in range(row_count)
            for c in range(col_count)
        ]
        recv.append(lax.ppermute(piece, ("row", "col"), pairs))
    stacked = jnp.stack(recv)
    own_value = sum(
        jnp.where((row_pos & mask) != 0, 1 << bit, 0) for bit, mask in enumerate(gather_masks)
    )
    return jnp.stack(
        [lax.dynamic_index_in_dim(stacked, u ^ own_value, 0, keepdims=False) for u in range(len(offsets))]
    )


def lower_inverse_from_blocks(factor, inv_diag, nb):
    inv = jnp.stack(inv_diag)
    size = nb
    while inv.shape[0] > 1:
        pair_count = inv.shape[0] // 2
        first_inv = inv[0::2]
        second_inv = inv[1::2]
        below = jnp.stack([
            factor[(2 * p + 1) * size:(2 * p + 2) * size, 2 * p * size:(2 * p + 1) * size]
            for p in range(pair_count)
        ])
        low = -jnp.einsum("pij,pjk,pkl->pil", second_inv, below, first_inv, precision=lax.Precision.HIGHEST)
        top = jnp.concatenate([first_inv, jnp.zeros_like(first_inv)], axis=2)
        bottom = jnp.concatenate([low, second_inv], axis=2)
        inv = jnp.concatenate([top, bottom], axis=1)
        size *= 2
    return inv[0]


def local(green, arrival, row_gauge, row_time, damping, trail):
    row_count = lax.axis_size("row")
    col_count = lax.axis_size("col")
    row_pos = lax.axis_index("row")
    col_pos = lax.axis_index("col")
    kq_rows, tile_rows, tile_width = green.shape
    panel_tiles = PANEL // NB
    far_slots = trail.shape[2]
    arrive = arrival[row_gauge][:, :, 0]
    is_live = row_time[:, None] >= arrive
    masked = jnp.where(is_live[:, :, None], green, jnp.zeros_like(green))
    flat_green = masked.reshape(kq_rows, tile_rows * tile_width)

    panel_holds = np.zeros((row_count, col_count), dtype=bool)
    panel_holds[:panel_tiles, :] = True
    panel_piece = spread_share(
        masked[:, 0, :], panel_holds, [[8, 32], [32, 8], [4, 16], [16, 4]], row_count, col_count
    )
    panel_pair = gather_share(panel_piece, (2,), row_count, col_count)
    panel_stack = gather_share(panel_pair, (1,), row_count, col_count)
    panel_cols = jnp.transpose(panel_stack, (2, 1, 0, 3)).reshape(kq_rows, PANEL)

    contract_rows = (((0,), (0,)), ((), ()))
    half = PANEL // 2
    core_bit = row_pos % 2
    diag_part = lax.dot_general(
        lax.dynamic_slice_in_dim(panel_cols, core_bit * half, half, 1),
        panel_cols, contract_rows, preferred_element_type=jnp.float32,
    )
    partial_value = lax.dot_general(
        flat_green, panel_cols, contract_rows, preferred_element_type=jnp.float32
    )
    diag_half = diag_part
    col_mask = 1
    while col_mask < col_count:
        col_pairs = [
            (r * col_count + c, r * col_count + (c ^ col_mask))
            for r in range(row_count)
            for c in range(col_count)
        ]
        diag_half = diag_half + lax.ppermute(diag_half, ("row", "col"), col_pairs)
        col_mask *= 2
    swap_pairs = [
        (r * col_count + c, (r ^ 1) * col_count + c)
        for r in range(row_count)
        for c in range(col_count)
    ]
    other_half = lax.ppermute(diag_half, ("row", "col"), swap_pairs)
    diag_block = jnp.where(
        core_bit == 0,
        jnp.concatenate([diag_half, other_half]),
        jnp.concatenate([other_half, diag_half]),
    )
    head_rows = partial_value[:tile_width]
    col_mask = 1
    while col_mask < col_count:
        col_pairs = [
            (r * col_count + c, r * col_count + (c ^ col_mask))
            for r in range(row_count)
            for c in range(col_count)
        ]
        head_rows = head_rows + lax.ppermute(head_rows, ("row", "col"), col_pairs)
        col_mask *= 2
    diag_block, rest_rows = lax.optimization_barrier((diag_block, partial_value[tile_width:]))
    normal_rows = jnp.concatenate([head_rows, lax.psum(rest_rows, "col")])

    far_holds = np.zeros((row_count, col_count), dtype=bool)
    for slot_no in range(far_slots):
        for c in range(col_count):
            far_holds[panel_tiles + slot_no * col_count + c, c] = True
    far_piece = spread_share(
        head_rows, far_holds, ((32,), (2,), (1,)), row_count, col_count
    )
    by_inverse = (((1,), (1,)), ((), ()))
    unit = jnp.eye(tile_width, dtype=jnp.float32)
    trailing = diag_block + jnp.diag(damping)
    factor_cols = []
    inv_diag = []
    for step in range(panel_tiles):
        head = trailing[:tile_width, :tile_width]
        head_factor = jnp.tril(jnp.linalg.cholesky(head))
        head_inv = lax.linalg.triangular_solve(head_factor, unit, left_side=True, lower=True)
        inv_diag.append(head_inv)
        if step + 1 < panel_tiles:
            panel = lax.dot_general(
                trailing[tile_width:, :tile_width], head_inv, by_inverse,
                precision=lax.Precision.HIGHEST, preferred_element_type=jnp.float32,
            )
            trailing = trailing[tile_width:, tile_width:] - lax.dot_general(
                panel, panel, by_inverse,
                precision=lax.Precision.HIGHEST, preferred_element_type=jnp.float32,
            )
            factor_cols.append(jnp.concatenate([head_factor, panel]))
        else:
            factor_cols.append(head_factor)
        if step == 0:
            trailing, far_piece = lax.optimization_barrier((trailing, far_piece))
            far_quad = gather_share(far_piece, (4, 8), row_count, col_count)
        if step == 2:
            trailing, far_quad = lax.optimization_barrier((trailing, far_quad))
            far_shared = gather_share(far_quad, (16,), row_count, col_count).reshape(
                far_slots, tile_width, PANEL
            )
    factor = jnp.concatenate(
        [jnp.pad(col, ((step * tile_width, 0), (0, 0))) for step, col in enumerate(factor_cols)],
        axis=1,
    )
    factor_inv = lower_inverse_from_blocks(factor, inv_diag, tile_width)
    factor_inv, far_shared = lax.optimization_barrier((factor_inv, far_shared))
    far_normal = jnp.roll(far_shared, -1, axis=0).reshape(far_slots * tile_width, PANEL)
    solved = lax.dot_general(
        normal_rows, factor_inv, by_inverse,
        precision=lax.Precision.HIGH, preferred_element_type=jnp.float32,
    )
    far_rows = lax.dot_general(
        far_normal, factor_inv, by_inverse,
        precision=lax.Precision.HIGH, preferred_element_type=jnp.float32,
    )
    solved = solved.reshape(tile_rows, tile_width, PANEL)
    tiles_list = []
    for local_no in range(tile_rows):
        tile_id = local_no * row_count + row_pos
        diag_rows = lax.dynamic_slice_in_dim(
            factor, jnp.minimum(tile_id, panel_tiles - 1) * tile_width, tile_width, 0
        )
        tiles_list.append(jnp.where(tile_id < panel_tiles, diag_rows, solved[local_no]))
    lower_rows = jnp.stack(tiles_list)
    col_share = PANEL // col_count
    chol_out = lax.dynamic_slice_in_dim(lower_rows, col_pos * col_share, col_share, 2)

    update = lax.dot_general(
        lower_rows.reshape(tile_rows * tile_width, PANEL),
        far_rows,
        (((1,), (1,)), ((), ())),
        precision=lax.Precision.HIGH,
        preferred_element_type=jnp.float32,
    )
    update = update.reshape(tile_rows, tile_width, far_slots, tile_width)
    tile_ids = jnp.arange(tile_rows, dtype=jnp.int32) * row_count + row_pos
    below_panel = (tile_ids >= panel_tiles)[:, None, None, None]
    return (chol_out, trail - jnp.where(below_panel, update, jnp.zeros_like(update)))


def solution(mesh):
    return jax.shard_map(
        local,
        mesh=mesh,
        in_specs=(
            P("col", None, "row"),
            P(None, None, "row"),
            P("col"),
            P("col"),
            P(),
            P(None, "row", None, "col"),
        ),
        out_specs=(P(None, "row", "col"), P(None, "row", None, "col")),
        check_vma=False,
    )
```

```python
import numpy as np
import jax
import jax.numpy as jnp
from jax import lax
from jax.sharding import PartitionSpec as P

NB = 128
PANEL = 512


def span_of(masks):
    values = [0]
    for mask in masks:
        values = values + [v ^ mask for v in values]
    return values


def spread_share(piece, holds, spread_rounds, row_count, col_count):
    row_pos = lax.axis_index("row")
    col_pos = lax.axis_index("col")
    flat_pos = row_pos * col_count + col_pos
    have = np.array(holds, dtype=bool)
    for round_masks in spread_rounds:
        gets_all = np.zeros_like(have)
        moved_list = []
        if isinstance(round_masks, list):
            mask_sets = [round_masks]
        else:
            mask_sets = [[mask, mask] for mask in span_of(round_masks)[1:]]
        for parity_masks in mask_sets:
            pairs = []
            gets = np.zeros_like(have)
            for r in range(row_count):
                mask = parity_masks[r % 2]
                for c in range(col_count):
                    if have[r, c] and not have[r ^ mask, c]:
                        pairs.append((r * col_count + c, (r ^ mask) * col_count + c))
                        gets[r ^ mask, c] = True
            assert not (gets & gets_all).any()
            gets_all = gets_all | gets
            moved_list.append((lax.ppermute(piece, ("row", "col"), pairs), gets))
        for moved, gets in moved_list:
            took = jnp.asarray(gets.reshape(-1))[flat_pos]
            piece = jnp.where(took, moved, piece)
        have = have | gets_all
    assert have.all()
    return piece


def gather_share(piece, gather_masks, row_count, col_count):
    row_pos = lax.axis_index("row")
    offsets = span_of(gather_masks)
    recv = [piece]
    for mask in offsets[1:]:
        pairs = [
            (r * col_count + c, (r ^ mask) * col_count + c)
            for r in range(row_count)
            for c in range(col_count)
        ]
        recv.append(lax.ppermute(piece, ("row", "col"), pairs))
    stacked = jnp.stack(recv)
    own_value = sum(
        jnp.where((row_pos & mask) != 0, 1 << bit, 0) for bit, mask in enumerate(gather_masks)
    )
    return jnp.stack(
        [lax.dynamic_index_in_dim(stacked, u ^ own_value, 0, keepdims=False) for u in range(len(offsets))]
    )


def lower_inverse_from_blocks(factor, inv_diag, nb):
    inv = jnp.stack(inv_diag)
    size = nb
    while inv.shape[0] > 1:
        pair_count = inv.shape[0] // 2
        first_inv = inv[0::2]
        second_inv = inv[1::2]
        below = jnp.stack([
            factor[(2 * p + 1) * size:(2 * p + 2) * size, 2 * p * size:(2 * p + 1) * size]
            for p in range(pair_count)
        ])
        low = -jnp.einsum("pij,pjk,pkl->pil", second_inv, below, first_inv, precision=lax.Precision.HIGHEST)
        top = jnp.concatenate([first_inv, jnp.zeros_like(first_inv)], axis=2)
        bottom = jnp.concatenate([low, second_inv], axis=2)
        inv = jnp.concatenate([top, bottom], axis=1)
        size *= 2
    return inv[0]


def local(green, arrival, row_gauge, row_time, damping, trail):
    row_count = lax.axis_size("row")
    col_count = lax.axis_size("col")
    row_pos = lax.axis_index("row")
    col_pos = lax.axis_index("col")
    kq_rows, tile_rows, tile_width = green.shape
    panel_tiles = PANEL // NB
    far_slots = trail.shape[2]
    arrive = arrival[row_gauge][:, :, 0]
    is_live = row_time[:, None] >= arrive
    masked = jnp.where(is_live[:, :, None], green, jnp.zeros_like(green))
    flat_green = masked.reshape(kq_rows, tile_rows * tile_width)

    panel_holds = np.zeros((row_count, col_count), dtype=bool)
    panel_holds[:panel_tiles, :] = True
    panel_piece = spread_share(
        masked[:, 0, :], panel_holds, [[8, 32], [32, 8], [4, 16], [16, 4]], row_count, col_count
    )
    panel_pair = gather_share(panel_piece, (2,), row_count, col_count)
    panel_stack = gather_share(panel_pair, (1,), row_count, col_count)
    panel_cols = jnp.transpose(panel_stack, (2, 1, 0, 3)).reshape(kq_rows, PANEL)

    contract_rows = (((0,), (0,)), ((), ()))
    half = PANEL // 2
    core_bit = row_pos % 2
    diag_part = lax.dot_general(
        lax.dynamic_slice_in_dim(panel_cols, core_bit * half, half, 1),
        panel_cols, contract_rows, preferred_element_type=jnp.float32,
    )
    partial_value = lax.dot_general(
        flat_green, panel_cols, contract_rows, preferred_element_type=jnp.float32
    )
    diag_half = diag_part
    col_mask = 1
    while col_mask < col_count:
        col_pairs = [
            (r * col_count + c, r * col_count + (c ^ col_mask))
            for r in range(row_count)
            for c in range(col_count)
        ]
        diag_half = diag_half + lax.ppermute(diag_half, ("row", "col"), col_pairs)
        col_mask *= 2
    swap_pairs = [
        (r * col_count + c, (r ^ 1) * col_count + c)
        for r in range(row_count)
        for c in range(col_count)
    ]
    other_half = lax.ppermute(diag_half, ("row", "col"), swap_pairs)
    diag_block = jnp.where(
        core_bit == 0,
        jnp.concatenate([diag_half, other_half]),
        jnp.concatenate([other_half, diag_half]),
    )
    head_rows = partial_value[:tile_width]
    col_mask = 1
    while col_mask < col_count:
        col_pairs = [
            (r * col_count + c, r * col_count + (c ^ col_mask))
            for r in range(row_count)
            for c in range(col_count)
        ]
        head_rows = head_rows + lax.ppermute(head_rows, ("row", "col"), col_pairs)
        col_mask *= 2
    diag_block, rest_rows = lax.optimization_barrier((diag_block, partial_value[tile_width:]))
    rest_sum = rest_rows

    far_holds = np.zeros((row_count, col_count), dtype=bool)
    for slot_no in range(far_slots):
        for c in range(col_count):
            far_holds[panel_tiles + slot_no * col_count + c, c] = True
    far_piece = spread_share(
        head_rows, far_holds, ((32,), (2,), (1,)), row_count, col_count
    )
    by_inverse = (((1,), (1,)), ((), ()))
    unit = jnp.eye(tile_width, dtype=jnp.float32)
    trailing = diag_block + jnp.diag(damping)
    factor_cols = []
    inv_diag = []
    for step in range(panel_tiles):
        head = trailing[:tile_width, :tile_width]
        head_factor = jnp.tril(jnp.linalg.cholesky(head))
        head_inv = lax.linalg.triangular_solve(head_factor, unit, left_side=True, lower=True)
        inv_diag.append(head_inv)
        if step + 1 < panel_tiles:
            panel = lax.dot_general(
                trailing[tile_width:, :tile_width], head_inv, by_inverse,
                precision=lax.Precision.HIGHEST, preferred_element_type=jnp.float32,
            )
            trailing = trailing[tile_width:, tile_width:] - lax.dot_general(
                panel, panel, by_inverse,
                precision=lax.Precision.HIGHEST, preferred_element_type=jnp.float32,
            )
            factor_cols.append(jnp.concatenate([head_factor, panel]))
        else:
            factor_cols.append(head_factor)
        if (1 << step) < col_count:
            trailing, far_piece, rest_sum = lax.optimization_barrier((trailing, far_piece, rest_sum))
            col_mask = 1 << step
            col_pairs = [
                (r * col_count + c, r * col_count + (c ^ col_mask))
                for r in range(row_count)
                for c in range(col_count)
            ]
            rest_sum = rest_sum + lax.ppermute(rest_sum, ("row", "col"), col_pairs)
        if step == 0:
            far_quad = gather_share(far_piece, (4, 8), row_count, col_count)
        if step == 2:
            trailing, far_quad, rest_sum = lax.optimization_barrier((trailing, far_quad, rest_sum))
            far_shared = gather_share(far_quad, (16,), row_count, col_count).reshape(
                far_slots, tile_width, PANEL
            )
    factor = jnp.concatenate(
        [jnp.pad(col, ((step * tile_width, 0), (0, 0))) for step, col in enumerate(factor_cols)],
        axis=1,
    )
    factor_inv = lower_inverse_from_blocks(factor, inv_diag, tile_width)
    factor_inv, far_shared = lax.optimization_barrier((factor_inv, far_shared))
    normal_rows = jnp.concatenate([head_rows, rest_sum])
    far_normal = jnp.roll(far_shared, -1, axis=0).reshape(far_slots * tile_width, PANEL)
    solved = lax.dot_general(
        normal_rows, factor_inv, by_inverse,
        precision=lax.Precision.HIGH, preferred_element_type=jnp.float32,
    )
    far_rows = lax.dot_general(
        far_normal, factor_inv, by_inverse,
        precision=lax.Precision.HIGH, preferred_element_type=jnp.float32,
    )
    solved = solved.reshape(tile_rows, tile_width, PANEL)
    tiles_list = []
    for local_no in range(tile_rows):
        tile_id = local_no * row_count + row_pos
        diag_rows = lax.dynamic_slice_in_dim(
            factor, jnp.minimum(tile_id, panel_tiles - 1) * tile_width, tile_width, 0
        )
        tiles_list.append(jnp.where(tile_id < panel_tiles, diag_rows, solved[local_no]))
    lower_rows = jnp.stack(tiles_list)
    col_share = PANEL // col_count
    chol_out = lax.dynamic_slice_in_dim(lower_rows, col_pos * col_share, col_share, 2)

    update = lax.dot_general(
        lower_rows.reshape(tile_rows * tile_width, PANEL),
        far_rows,
        (((1,), (1,)), ((), ())),
        precision=lax.Precision.HIGH,
        preferred_element_type=jnp.float32,
    )
    update = update.reshape(tile_rows, tile_width, far_slots, tile_width)
    tile_ids = jnp.arange(tile_rows, dtype=jnp.int32) * row_count + row_pos
    below_panel = (tile_ids >= panel_tiles)[:, None, None, None]
    return (chol_out, trail - jnp.where(below_panel, update, jnp.zeros_like(update)))


def solution(mesh):
    return jax.shard_map(
        local,
        mesh=mesh,
        in_specs=(
            P("col", None, "row"),
            P(None, None, "row"),
            P("col"),
            P("col"),
            P(),
            P(None, "row", None, "col"),
        ),
        out_specs=(P(None, "row", "col"), P(None, "row", None, "col")),
        check_vma=False,
    )
```

```python
import numpy as np
import jax
import jax.numpy as jnp
from jax import lax
from jax.sharding import PartitionSpec as P

NB = 128
PANEL = 512


def span_of(masks):
    values = [0]
    for mask in masks:
        values = values + [v ^ mask for v in values]
    return values


def spread_share(piece, holds, spread_rounds, row_count, col_count):
    row_pos = lax.axis_index("row")
    col_pos = lax.axis_index("col")
    flat_pos = row_pos * col_count + col_pos
    have = np.array(holds, dtype=bool)
    for round_masks in spread_rounds:
        gets_all = np.zeros_like(have)
        moved_list = []
        if isinstance(round_masks, list):
            mask_sets = [round_masks]
        else:
            mask_sets = [[mask, mask] for mask in span_of(round_masks)[1:]]
        for parity_masks in mask_sets:
            pairs = []
            gets = np.zeros_like(have)
            for r in range(row_count):
                mask = parity_masks[r % 2]
                for c in range(col_count):
                    if have[r, c] and not have[r ^ mask, c]:
                        pairs.append((r * col_count + c, (r ^ mask) * col_count + c))
                        gets[r ^ mask, c] = True
            assert not (gets & gets_all).any()
            gets_all = gets_all | gets
            moved_list.append((lax.ppermute(piece, ("row", "col"), pairs), gets))
        for moved, gets in moved_list:
            took = jnp.asarray(gets.reshape(-1))[flat_pos]
            piece = jnp.where(took, moved, piece)
        have = have | gets_all
    assert have.all()
    return piece


def gather_share(piece, gather_masks, row_count, col_count):
    row_pos = lax.axis_index("row")
    offsets = span_of(gather_masks)
    recv = [piece]
    for mask in offsets[1:]:
        pairs = [
            (r * col_count + c, (r ^ mask) * col_count + c)
            for r in range(row_count)
            for c in range(col_count)
        ]
        recv.append(lax.ppermute(piece, ("row", "col"), pairs))
    stacked = jnp.stack(recv)
    own_value = sum(
        jnp.where((row_pos & mask) != 0, 1 << bit, 0) for bit, mask in enumerate(gather_masks)
    )
    return jnp.stack(
        [lax.dynamic_index_in_dim(stacked, u ^ own_value, 0, keepdims=False) for u in range(len(offsets))]
    )


def lower_inverse_from_blocks(factor, inv_diag, nb):
    inv = jnp.stack(inv_diag)
    size = nb
    while inv.shape[0] > 1:
        pair_count = inv.shape[0] // 2
        first_inv = inv[0::2]
        second_inv = inv[1::2]
        below = jnp.stack([
            factor[(2 * p + 1) * size:(2 * p + 2) * size, 2 * p * size:(2 * p + 1) * size]
            for p in range(pair_count)
        ])
        low = -jnp.einsum("pij,pjk,pkl->pil", second_inv, below, first_inv, precision=lax.Precision.HIGHEST)
        top = jnp.concatenate([first_inv, jnp.zeros_like(first_inv)], axis=2)
        bottom = jnp.concatenate([low, second_inv], axis=2)
        inv = jnp.concatenate([top, bottom], axis=1)
        size *= 2
    return inv[0]


def local(green, arrival, row_gauge, row_time, damping, trail):
    row_count = lax.axis_size("row")
    col_count = lax.axis_size("col")
    row_pos = lax.axis_index("row")
    col_pos = lax.axis_index("col")
    kq_rows, tile_rows, tile_width = green.shape
    panel_tiles = PANEL // NB
    far_slots = trail.shape[2]
    arrive = arrival[row_gauge][:, :, 0]
    is_live = row_time[:, None] >= arrive
    masked = jnp.where(is_live[:, :, None], green, jnp.zeros_like(green))
    flat_green = masked.reshape(kq_rows, tile_rows * tile_width)

    panel_holds = np.zeros((row_count, col_count), dtype=bool)
    panel_holds[:panel_tiles, :] = True
    panel_piece = spread_share(
        masked[:, 0, :], panel_holds, [[8, 32], [32, 8], [4, 16], [16, 4]], row_count, col_count
    )
    panel_pair = gather_share(panel_piece, (2,), row_count, col_count)
    panel_stack = gather_share(panel_pair, (1,), row_count, col_count)
    panel_cols = jnp.transpose(panel_stack, (2, 1, 0, 3)).reshape(kq_rows, PANEL)

    contract_rows = (((0,), (0,)), ((), ()))
    half = PANEL // 2
    core_bit = row_pos % 2
    diag_part = lax.dot_general(
        lax.dynamic_slice_in_dim(panel_cols, core_bit * half, half, 1),
        panel_cols, contract_rows, preferred_element_type=jnp.float32,
    )
    partial_value = lax.dot_general(
        flat_green, panel_cols, contract_rows, preferred_element_type=jnp.float32
    )
    diag_half = diag_part
    col_mask = 1
    while col_mask < col_count:
        col_pairs = [
            (r * col_count + c, r * col_count + (c ^ col_mask))
            for r in range(row_count)
            for c in range(col_count)
        ]
        diag_half = diag_half + lax.ppermute(diag_half, ("row", "col"), col_pairs)
        col_mask *= 2
    swap_pairs = [
        (r * col_count + c, (r ^ 1) * col_count + c)
        for r in range(row_count)
        for c in range(col_count)
    ]
    other_half = lax.ppermute(diag_half, ("row", "col"), swap_pairs)
    diag_block = jnp.where(
        core_bit == 0,
        jnp.concatenate([diag_half, other_half]),
        jnp.concatenate([other_half, diag_half]),
    )
    diag_block, rest_rows, head_rows = lax.optimization_barrier(
        (diag_block, partial_value[tile_width:], partial_value[:tile_width])
    )
    col_mask = 1
    while col_mask < col_count:
        col_pairs = [
            (r * col_count + c, r * col_count + (c ^ col_mask))
            for r in range(row_count)
            for c in range(col_count)
        ]
        head_rows = head_rows + lax.ppermute(head_rows, ("row", "col"), col_pairs)
        col_mask *= 2
    rest_sum = rest_rows

    far_holds = np.zeros((row_count, col_count), dtype=bool)
    for slot_no in range(far_slots):
        for c in range(col_count):
            far_holds[panel_tiles + slot_no * col_count + c, c] = True
    far_piece = spread_share(
        head_rows, far_holds, ((32,), (2,), (1,)), row_count, col_count
    )
    by_inverse = (((1,), (1,)), ((), ()))
    unit = jnp.eye(tile_width, dtype=jnp.float32)
    trailing = diag_block + jnp.diag(damping)
    factor_cols = []
    inv_diag = []
    for step in range(panel_tiles):
        head = trailing[:tile_width, :tile_width]
        head_factor = jnp.tril(jnp.linalg.cholesky(head))
        head_inv = lax.linalg.triangular_solve(head_factor, unit, left_side=True, lower=True)
        inv_diag.append(head_inv)
        if step + 1 < panel_tiles:
            panel = lax.dot_general(
                trailing[tile_width:, :tile_width], head_inv, by_inverse,
                precision=lax.Precision.HIGHEST, preferred_element_type=jnp.float32,
            )
            trailing = trailing[tile_width:, tile_width:] - lax.dot_general(
                panel, panel, by_inverse,
                precision=lax.Precision.HIGHEST, preferred_element_type=jnp.float32,
            )
            factor_cols.append(jnp.concatenate([head_factor, panel]))
        else:
            factor_cols.append(head_factor)
        if (1 << step) < col_count:
            trailing, far_piece, rest_sum = lax.optimization_barrier((trailing, far_piece, rest_sum))
            col_mask = 1 << step
            col_pairs = [
                (r * col_count + c, r * col_count + (c ^ col_mask))
                for r in range(row_count)
                for c in range(col_count)
            ]
            rest_sum = rest_sum + lax.ppermute(rest_sum, ("row", "col"), col_pairs)
        if step == 1:
            far_quad = gather_share(far_piece, (4, 8), row_count, col_count)
        if step == 2:
            trailing, far_quad, rest_sum = lax.optimization_barrier((trailing, far_quad, rest_sum))
            far_shared = gather_share(far_quad, (16,), row_count, col_count).reshape(
                far_slots, tile_width, PANEL
            )
    factor = jnp.concatenate(
        [jnp.pad(col, ((step * tile_width, 0), (0, 0))) for step, col in enumerate(factor_cols)],
        axis=1,
    )
    factor_inv = lower_inverse_from_blocks(factor, inv_diag, tile_width)
    factor_inv, far_shared = lax.optimization_barrier((factor_inv, far_shared))
    normal_rows = jnp.concatenate([head_rows, rest_sum])
    far_normal = jnp.roll(far_shared, -1, axis=0).reshape(far_slots * tile_width, PANEL)
    solved = lax.dot_general(
        normal_rows, factor_inv, by_inverse,
        precision=lax.Precision.HIGH, preferred_element_type=jnp.float32,
    )
    far_rows = lax.dot_general(
        far_normal, factor_inv, by_inverse,
        precision=lax.Precision.HIGH, preferred_element_type=jnp.float32,
    )
    solved = solved.reshape(tile_rows, tile_width, PANEL)
    tiles_list = []
    for local_no in range(tile_rows):
        tile_id = local_no * row_count + row_pos
        diag_rows = lax.dynamic_slice_in_dim(
            factor, jnp.minimum(tile_id, panel_tiles - 1) * tile_width, tile_width, 0
        )
        tiles_list.append(jnp.where(tile_id < panel_tiles, diag_rows, solved[local_no]))
    lower_rows = jnp.stack(tiles_list)
    col_share = PANEL // col_count
    chol_out = lax.dynamic_slice_in_dim(lower_rows, col_pos * col_share, col_share, 2)

    update = lax.dot_general(
        lower_rows.reshape(tile_rows * tile_width, PANEL),
        far_rows,
        (((1,), (1,)), ((), ())),
        precision=lax.Precision.HIGH,
        preferred_element_type=jnp.float32,
    )
    update = update.reshape(tile_rows, tile_width, far_slots, tile_width)
    tile_ids = jnp.arange(tile_rows, dtype=jnp.int32) * row_count + row_pos
    below_panel = (tile_ids >= panel_tiles)[:, None, None, None]
    return (chol_out, trail - jnp.where(below_panel, update, jnp.zeros_like(update)))


def solution(mesh):
    return jax.shard_map(
        local,
        mesh=mesh,
        in_specs=(
            P("col", None, "row"),
            P(None, None, "row"),
            P("col"),
            P("col"),
            P(),
            P(None, "row", None, "col"),
        ),
        out_specs=(P(None, "row", "col"), P(None, "row", None, "col")),
        check_vma=False,
    )
```

```python
import numpy as np
import jax
import jax.numpy as jnp
from jax import lax
from jax.sharding import PartitionSpec as P

NB = 128
PANEL = 512


def span_of(masks):
    values = [0]
    for mask in masks:
        values = values + [v ^ mask for v in values]
    return values


def spread_share(piece, holds, spread_rounds, row_count, col_count):
    row_pos = lax.axis_index("row")
    col_pos = lax.axis_index("col")
    flat_pos = row_pos * col_count + col_pos
    have = np.array(holds, dtype=bool)
    for round_masks in spread_rounds:
        gets_all = np.zeros_like(have)
        moved_list = []
        if isinstance(round_masks, list):
            mask_sets = [round_masks]
        else:
            mask_sets = [[mask, mask] for mask in span_of(round_masks)[1:]]
        for parity_masks in mask_sets:
            pairs = []
            gets = np.zeros_like(have)
            for r in range(row_count):
                mask = parity_masks[r % 2]
                for c in range(col_count):
                    if have[r, c] and not have[r ^ mask, c]:
                        pairs.append((r * col_count + c, (r ^ mask) * col_count + c))
                        gets[r ^ mask, c] = True
            assert not (gets & gets_all).any()
            gets_all = gets_all | gets
            moved_list.append((lax.ppermute(piece, ("row", "col"), pairs), gets))
        for moved, gets in moved_list:
            took = jnp.asarray(gets.reshape(-1))[flat_pos]
            piece = jnp.where(took, moved, piece)
        have = have | gets_all
    assert have.all()
    return piece


def gather_share(piece, gather_masks, row_count, col_count):
    row_pos = lax.axis_index("row")
    offsets = span_of(gather_masks)
    recv = [piece]
    for mask in offsets[1:]:
        pairs = [
            (r * col_count + c, (r ^ mask) * col_count + c)
            for r in range(row_count)
            for c in range(col_count)
        ]
        recv.append(lax.ppermute(piece, ("row", "col"), pairs))
    stacked = jnp.stack(recv)
    own_value = sum(
        jnp.where((row_pos & mask) != 0, 1 << bit, 0) for bit, mask in enumerate(gather_masks)
    )
    return jnp.stack(
        [lax.dynamic_index_in_dim(stacked, u ^ own_value, 0, keepdims=False) for u in range(len(offsets))]
    )


def lower_inverse_from_blocks(factor, inv_diag, nb):
    inv = jnp.stack(inv_diag)
    size = nb
    while inv.shape[0] > 1:
        pair_count = inv.shape[0] // 2
        first_inv = inv[0::2]
        second_inv = inv[1::2]
        below = jnp.stack([
            factor[(2 * p + 1) * size:(2 * p + 2) * size, 2 * p * size:(2 * p + 1) * size]
            for p in range(pair_count)
        ])
        low = -jnp.einsum("pij,pjk,pkl->pil", second_inv, below, first_inv, precision=lax.Precision.HIGHEST)
        top = jnp.concatenate([first_inv, jnp.zeros_like(first_inv)], axis=2)
        bottom = jnp.concatenate([low, second_inv], axis=2)
        inv = jnp.concatenate([top, bottom], axis=1)
        size *= 2
    return inv[0]


def local(green, arrival, row_gauge, row_time, damping, trail):
    row_count = lax.axis_size("row")
    col_count = lax.axis_size("col")
    row_pos = lax.axis_index("row")
    col_pos = lax.axis_index("col")
    kq_rows, tile_rows, tile_width = green.shape
    panel_tiles = PANEL // NB
    far_slots = trail.shape[2]
    arrive = arrival[row_gauge][:, :, 0]
    is_live = row_time[:, None] >= arrive
    masked = jnp.where(is_live[:, :, None], green, jnp.zeros_like(green))
    flat_green = masked.reshape(kq_rows, tile_rows * tile_width)

    panel_holds = np.zeros((row_count, col_count), dtype=bool)
    panel_holds[:panel_tiles, :] = True
    panel_piece = spread_share(
        masked[:, 0, :], panel_holds, [[8, 32], [32, 8], [4, 16], [16, 4]], row_count, col_count
    )
    panel_pair = gather_share(panel_piece, (2,), row_count, col_count)
    panel_stack = gather_share(panel_pair, (1,), row_count, col_count)
    panel_cols = jnp.transpose(panel_stack, (2, 1, 0, 3)).reshape(kq_rows, PANEL)

    if col_count == 4:
        col_masks = (1, 3)
    else:
        col_masks = tuple(1 << b for b in range(col_count.bit_length() - 1))
    contract_rows = (((0,), (0,)), ((), ()))
    half = PANEL // 2
    core_bit = row_pos % 2
    diag_part = lax.dot_general(
        lax.dynamic_slice_in_dim(panel_cols, core_bit * half, half, 1),
        panel_cols, contract_rows, preferred_element_type=jnp.float32,
    )
    partial_value = lax.dot_general(
        flat_green, panel_cols, contract_rows, preferred_element_type=jnp.float32
    )
    diag_half = diag_part
    for col_mask in col_masks:
        col_pairs = [
            (r * col_count + c, r * col_count + (c ^ col_mask))
            for r in range(row_count)
            for c in range(col_count)
        ]
        diag_half = diag_half + lax.ppermute(diag_half, ("row", "col"), col_pairs)
    swap_pairs = [
        (r * col_count + c, (r ^ 1) * col_count + c)
        for r in range(row_count)
        for c in range(col_count)
    ]
    other_half = lax.ppermute(diag_half, ("row", "col"), swap_pairs)
    diag_block = jnp.where(
        core_bit == 0,
        jnp.concatenate([diag_half, other_half]),
        jnp.concatenate([other_half, diag_half]),
    )
    head_rows = partial_value[:tile_width]
    for col_mask in col_masks:
        col_pairs = [
            (r * col_count + c, r * col_count + (c ^ col_mask))
            for r in range(row_count)
            for c in range(col_count)
        ]
        head_rows = head_rows + lax.ppermute(head_rows, ("row", "col"), col_pairs)
    diag_block, rest_rows = lax.optimization_barrier((diag_block, partial_value[tile_width:]))
    rest_sum = rest_rows

    far_holds = np.zeros((row_count, col_count), dtype=bool)
    for slot_no in range(far_slots):
        for c in range(col_count):
            far_holds[panel_tiles + slot_no * col_count + c, c] = True
    far_piece = spread_share(
        head_rows, far_holds, ((32,), (2,), (1,)), row_count, col_count
    )
    by_inverse = (((1,), (1,)), ((), ()))
    unit = jnp.eye(tile_width, dtype=jnp.float32)
    trailing = diag_block + jnp.diag(damping)
    factor_cols = []
    inv_diag = []
    for step in range(panel_tiles):
        head = trailing[:tile_width, :tile_width]
        head_factor = jnp.tril(jnp.linalg.cholesky(head))
        head_inv = lax.linalg.triangular_solve(head_factor, unit, left_side=True, lower=True)
        inv_diag.append(head_inv)
        if step + 1 < panel_tiles:
            panel = lax.dot_general(
                trailing[tile_width:, :tile_width], head_inv, by_inverse,
                precision=lax.Precision.HIGHEST, preferred_element_type=jnp.float32,
            )
            trailing = trailing[tile_width:, tile_width:] - lax.dot_general(
                panel, panel, by_inverse,
                precision=lax.Precision.HIGHEST, preferred_element_type=jnp.float32,
            )
            factor_cols.append(jnp.concatenate([head_factor, panel]))
        else:
            factor_cols.append(head_factor)
        if step < len(col_masks):
            trailing, far_piece, rest_sum = lax.optimization_barrier((trailing, far_piece, rest_sum))
            col_mask = col_masks[step]
            col_pairs = [
                (r * col_count + c, r * col_count + (c ^ col_mask))
                for r in range(row_count)
                for c in range(col_count)
            ]
            rest_sum = rest_sum + lax.ppermute(rest_sum, ("row", "col"), col_pairs)
        if step == 0:
            far_quad = gather_share(far_piece, (4, 8), row_count, col_count)
        if step == 2:
            trailing, far_quad, rest_sum = lax.optimization_barrier((trailing, far_quad, rest_sum))
            far_shared = gather_share(far_quad, (16,), row_count, col_count).reshape(
                far_slots, tile_width, PANEL
            )
    factor = jnp.concatenate(
        [jnp.pad(col, ((step * tile_width, 0), (0, 0))) for step, col in enumerate(factor_cols)],
        axis=1,
    )
    factor_inv = lower_inverse_from_blocks(factor, inv_diag, tile_width)
    factor_inv, far_shared = lax.optimization_barrier((factor_inv, far_shared))
    normal_rows = jnp.concatenate([head_rows, rest_sum])
    far_normal = jnp.roll(far_shared, -1, axis=0).reshape(far_slots * tile_width, PANEL)
    solved = lax.dot_general(
        normal_rows, factor_inv, by_inverse,
        precision=lax.Precision.HIGH, preferred_element_type=jnp.float32,
    )
    far_rows = lax.dot_general(
        far_normal, factor_inv, by_inverse,
        precision=lax.Precision.HIGH, preferred_element_type=jnp.float32,
    )
    solved = solved.reshape(tile_rows, tile_width, PANEL)
    tiles_list = []
    for local_no in range(tile_rows):
        tile_id = local_no * row_count + row_pos
        diag_rows = lax.dynamic_slice_in_dim(
            factor, jnp.minimum(tile_id, panel_tiles - 1) * tile_width, tile_width, 0
        )
        tiles_list.append(jnp.where(tile_id < panel_tiles, diag_rows, solved[local_no]))
    lower_rows = jnp.stack(tiles_list)
    col_share = PANEL // col_count
    chol_out = lax.dynamic_slice_in_dim(lower_rows, col_pos * col_share, col_share, 2)

    update = lax.dot_general(
        lower_rows.reshape(tile_rows * tile_width, PANEL),
        far_rows,
        (((1,), (1,)), ((), ())),
        precision=lax.Precision.HIGH,
        preferred_element_type=jnp.float32,
    )
    update = update.reshape(tile_rows, tile_width, far_slots, tile_width)
    tile_ids = jnp.arange(tile_rows, dtype=jnp.int32) * row_count + row_pos
    below_panel = (tile_ids >= panel_tiles)[:, None, None, None]
    return (chol_out, trail - jnp.where(below_panel, update, jnp.zeros_like(update)))


def solution(mesh):
    return jax.shard_map(
        local,
        mesh=mesh,
        in_specs=(
            P("col", None, "row"),
            P(None, None, "row"),
            P("col"),
            P("col"),
            P(),
            P(None, "row", None, "col"),
        ),
        out_specs=(P(None, "row", "col"), P(None, "row", None, "col")),
        check_vma=False,
    )
```

```python
import numpy as np
import jax
import jax.numpy as jnp
from jax import lax
from jax.sharding import PartitionSpec as P

NB = 128
PANEL = 512


def span_of(masks):
    values = [0]
    for mask in masks:
        values = values + [v ^ mask for v in values]
    return values


def spread_share(piece, holds, spread_rounds, row_count, col_count):
    row_pos = lax.axis_index("row")
    col_pos = lax.axis_index("col")
    flat_pos = row_pos * col_count + col_pos
    have = np.array(holds, dtype=bool)
    for round_masks in spread_rounds:
        gets_all = np.zeros_like(have)
        moved_list = []
        if isinstance(round_masks, list):
            mask_sets = [round_masks]
        else:
            mask_sets = [[mask, mask] for mask in span_of(round_masks)[1:]]
        for parity_masks in mask_sets:
            pairs = []
            gets = np.zeros_like(have)
            for r in range(row_count):
                mask = parity_masks[r % 2]
                for c in range(col_count):
                    if have[r, c] and not have[r ^ mask, c]:
                        pairs.append((r * col_count + c, (r ^ mask) * col_count + c))
                        gets[r ^ mask, c] = True
            assert not (gets & gets_all).any()
            gets_all = gets_all | gets
            moved_list.append((lax.ppermute(piece, ("row", "col"), pairs), gets))
        for moved, gets in moved_list:
            took = jnp.asarray(gets.reshape(-1))[flat_pos]
            piece = jnp.where(took, moved, piece)
        have = have | gets_all
    assert have.all()
    return piece


def gather_share(piece, gather_masks, row_count, col_count):
    row_pos = lax.axis_index("row")
    offsets = span_of(gather_masks)
    recv = [piece]
    for mask in offsets[1:]:
        pairs = [
            (r * col_count + c, (r ^ mask) * col_count + c)
            for r in range(row_count)
            for c in range(col_count)
        ]
        recv.append(lax.ppermute(piece, ("row", "col"), pairs))
    stacked = jnp.stack(recv)
    own_value = sum(
        jnp.where((row_pos & mask) != 0, 1 << bit, 0) for bit, mask in enumerate(gather_masks)
    )
    return jnp.stack(
        [lax.dynamic_index_in_dim(stacked, u ^ own_value, 0, keepdims=False) for u in range(len(offsets))]
    )


def lower_inverse_from_blocks(factor, inv_diag, nb):
    inv = jnp.stack(inv_diag)
    size = nb
    while inv.shape[0] > 1:
        pair_count = inv.shape[0] // 2
        first_inv = inv[0::2]
        second_inv = inv[1::2]
        below = jnp.stack([
            factor[(2 * p + 1) * size:(2 * p + 2) * size, 2 * p * size:(2 * p + 1) * size]
            for p in range(pair_count)
        ])
        low = -jnp.einsum("pij,pjk,pkl->pil", second_inv, below, first_inv, precision=lax.Precision.HIGHEST)
        top = jnp.concatenate([first_inv, jnp.zeros_like(first_inv)], axis=2)
        bottom = jnp.concatenate([low, second_inv], axis=2)
        inv = jnp.concatenate([top, bottom], axis=1)
        size *= 2
    return inv[0]


def local(green, arrival, row_gauge, row_time, damping, trail):
    row_count = lax.axis_size("row")
    col_count = lax.axis_size("col")
    row_pos = lax.axis_index("row")
    col_pos = lax.axis_index("col")
    kq_rows, tile_rows, tile_width = green.shape
    panel_tiles = PANEL // NB
    far_slots = trail.shape[2]
    arrive = arrival[row_gauge][:, :, 0]
    is_live = row_time[:, None] >= arrive
    masked = jnp.where(is_live[:, :, None], green, jnp.zeros_like(green))
    flat_green = masked.reshape(kq_rows, tile_rows * tile_width)

    panel_holds = np.zeros((row_count, col_count), dtype=bool)
    panel_holds[:panel_tiles, :] = True
    panel_piece = spread_share(
        masked[:, 0, :], panel_holds, [[12, 48], [48, 12], [4, 16], [16, 4]], row_count, col_count
    )
    panel_pair = gather_share(panel_piece, (2,), row_count, col_count)
    panel_stack = gather_share(panel_pair, (1,), row_count, col_count)
    panel_cols = jnp.transpose(panel_stack, (2, 1, 0, 3)).reshape(kq_rows, PANEL)

    if col_count == 4:
        col_masks = (1, 3)
    else:
        col_masks = tuple(1 << b for b in range(col_count.bit_length() - 1))
    contract_rows = (((0,), (0,)), ((), ()))
    half = PANEL // 2
    core_bit = row_pos % 2
    diag_part = lax.dot_general(
        lax.dynamic_slice_in_dim(panel_cols, core_bit * half, half, 1),
        panel_cols, contract_rows, preferred_element_type=jnp.float32,
    )
    partial_value = lax.dot_general(
        flat_green, panel_cols, contract_rows, preferred_element_type=jnp.float32
    )
    diag_half = diag_part
    for col_mask in col_masks:
        col_pairs = [
            (r * col_count + c, r * col_count + (c ^ col_mask))
            for r in range(row_count)
            for c in range(col_count)
        ]
        diag_half = diag_half + lax.ppermute(diag_half, ("row", "col"), col_pairs)
    swap_pairs = [
        (r * col_count + c, (r ^ 1) * col_count + c)
        for r in range(row_count)
        for c in range(col_count)
    ]
    other_half = lax.ppermute(diag_half, ("row", "col"), swap_pairs)
    diag_block = jnp.where(
        core_bit == 0,
        jnp.concatenate([diag_half, other_half]),
        jnp.concatenate([other_half, diag_half]),
    )
    head_rows = partial_value[:tile_width]
    for col_mask in col_masks:
        col_pairs = [
            (r * col_count + c, r * col_count + (c ^ col_mask))
            for r in range(row_count)
            for c in range(col_count)
        ]
        head_rows = head_rows + lax.ppermute(head_rows, ("row", "col"), col_pairs)
    diag_block, rest_rows = lax.optimization_barrier((diag_block, partial_value[tile_width:]))
    rest_sum = rest_rows

    far_holds = np.zeros((row_count, col_count), dtype=bool)
    for slot_no in range(far_slots):
        for c in range(col_count):
            far_holds[panel_tiles + slot_no * col_count + c, c] = True
    far_piece = spread_share(
        head_rows, far_holds, ((32,), (2,), (1,)), row_count, col_count
    )
    by_inverse = (((1,), (1,)), ((), ()))
    unit = jnp.eye(tile_width, dtype=jnp.float32)
    trailing = diag_block + jnp.diag(damping)
    factor_cols = []
    inv_diag = []
    for step in range(panel_tiles):
        head = trailing[:tile_width, :tile_width]
        head_factor = jnp.tril(jnp.linalg.cholesky(head))
        head_inv = lax.linalg.triangular_solve(head_factor, unit, left_side=True, lower=True)
        inv_diag.append(head_inv)
        if step + 1 < panel_tiles:
            panel = lax.dot_general(
                trailing[tile_width:, :tile_width], head_inv, by_inverse,
                precision=lax.Precision.HIGHEST, preferred_element_type=jnp.float32,
            )
            trailing = trailing[tile_width:, tile_width:] - lax.dot_general(
                panel, panel, by_inverse,
                precision=lax.Precision.HIGHEST, preferred_element_type=jnp.float32,
            )
            factor_cols.append(jnp.concatenate([head_factor, panel]))
        else:
            factor_cols.append(head_factor)
        if step < len(col_masks):
            trailing, far_piece, rest_sum = lax.optimization_barrier((trailing, far_piece, rest_sum))
            col_mask = col_masks[step]
            col_pairs = [
                (r * col_count + c, r * col_count + (c ^ col_mask))
                for r in range(row_count)
                for c in range(col_count)
            ]
            rest_sum = rest_sum + lax.ppermute(rest_sum, ("row", "col"), col_pairs)
        if step == 0:
            far_quad = gather_share(far_piece, (4, 8), row_count, col_count)
        if step == 2:
            trailing, far_quad, rest_sum = lax.optimization_barrier((trailing, far_quad, rest_sum))
            far_shared = gather_share(far_quad, (16,), row_count, col_count).reshape(
                far_slots, tile_width, PANEL
            )
    factor = jnp.concatenate(
        [jnp.pad(col, ((step * tile_width, 0), (0, 0))) for step, col in enumerate(factor_cols)],
        axis=1,
    )
    factor_inv = lower_inverse_from_blocks(factor, inv_diag, tile_width)
    factor_inv, far_shared = lax.optimization_barrier((factor_inv, far_shared))
    normal_rows = jnp.concatenate([head_rows, rest_sum])
    far_normal = jnp.roll(far_shared, -1, axis=0).reshape(far_slots * tile_width, PANEL)
    solved = lax.dot_general(
        normal_rows, factor_inv, by_inverse,
        precision=lax.Precision.HIGH, preferred_element_type=jnp.float32,
    )
    far_rows = lax.dot_general(
        far_normal, factor_inv, by_inverse,
        precision=lax.Precision.HIGH, preferred_element_type=jnp.float32,
    )
    solved = solved.reshape(tile_rows, tile_width, PANEL)
    tiles_list = []
    for local_no in range(tile_rows):
        tile_id = local_no * row_count + row_pos
        diag_rows = lax.dynamic_slice_in_dim(
            factor, jnp.minimum(tile_id, panel_tiles - 1) * tile_width, tile_width, 0
        )
        tiles_list.append(jnp.where(tile_id < panel_tiles, diag_rows, solved[local_no]))
    lower_rows = jnp.stack(tiles_list)
    col_share = PANEL // col_count
    chol_out = lax.dynamic_slice_in_dim(lower_rows, col_pos * col_share, col_share, 2)

    update = lax.dot_general(
        lower_rows.reshape(tile_rows * tile_width, PANEL),
        far_rows,
        (((1,), (1,)), ((), ())),
        precision=lax.Precision.HIGH,
        preferred_element_type=jnp.float32,
    )
    update = update.reshape(tile_rows, tile_width, far_slots, tile_width)
    tile_ids = jnp.arange(tile_rows, dtype=jnp.int32) * row_count + row_pos
    below_panel = (tile_ids >= panel_tiles)[:, None, None, None]
    return (chol_out, trail - jnp.where(below_panel, update, jnp.zeros_like(update)))


def solution(mesh):
    return jax.shard_map(
        local,
        mesh=mesh,
        in_specs=(
            P("col", None, "row"),
            P(None, None, "row"),
            P("col"),
            P("col"),
            P(),
            P(None, "row", None, "col"),
        ),
        out_specs=(P(None, "row", "col"), P(None, "row", None, "col")),
        check_vma=False,
    )
```

```python
import numpy as np
import jax
import jax.numpy as jnp
from jax import lax
from jax.sharding import PartitionSpec as P

NB = 128
PANEL = 512


def span_of(masks):
    values = [0]
    for mask in masks:
        values = values + [v ^ mask for v in values]
    return values


def spread_share(piece, holds, spread_rounds, row_count, col_count):
    row_pos = lax.axis_index("row")
    col_pos = lax.axis_index("col")
    flat_pos = row_pos * col_count + col_pos
    have = np.array(holds, dtype=bool)
    for round_masks in spread_rounds:
        gets_all = np.zeros_like(have)
        moved_list = []
        if isinstance(round_masks, list):
            mask_sets = [round_masks]
        else:
            mask_sets = [[mask, mask] for mask in span_of(round_masks)[1:]]
        for parity_masks in mask_sets:
            pairs = []
            gets = np.zeros_like(have)
            for r in range(row_count):
                mask = parity_masks[r % 2]
                for c in range(col_count):
                    if have[r, c] and not have[r ^ mask, c]:
                        pairs.append((r * col_count + c, (r ^ mask) * col_count + c))
                        gets[r ^ mask, c] = True
            assert not (gets & gets_all).any()
            gets_all = gets_all | gets
            moved_list.append((lax.ppermute(piece, ("row", "col"), pairs), gets))
        for moved, gets in moved_list:
            took = jnp.asarray(gets.reshape(-1))[flat_pos]
            piece = jnp.where(took, moved, piece)
        have = have | gets_all
    assert have.all()
    return piece


def gather_share(piece, gather_masks, row_count, col_count):
    row_pos = lax.axis_index("row")
    offsets = span_of(gather_masks)
    recv = [piece]
    for mask in offsets[1:]:
        pairs = [
            (r * col_count + c, (r ^ mask) * col_count + c)
            for r in range(row_count)
            for c in range(col_count)
        ]
        recv.append(lax.ppermute(piece, ("row", "col"), pairs))
    stacked = jnp.stack(recv)
    own_value = sum(
        jnp.where((row_pos & mask) != 0, 1 << bit, 0) for bit, mask in enumerate(gather_masks)
    )
    return jnp.stack(
        [lax.dynamic_index_in_dim(stacked, u ^ own_value, 0, keepdims=False) for u in range(len(offsets))]
    )


def lower_inverse_from_blocks(factor, inv_diag, nb):
    inv = jnp.stack(inv_diag)
    size = nb
    while inv.shape[0] > 1:
        pair_count = inv.shape[0] // 2
        first_inv = inv[0::2]
        second_inv = inv[1::2]
        below = jnp.stack([
            factor[(2 * p + 1) * size:(2 * p + 2) * size, 2 * p * size:(2 * p + 1) * size]
            for p in range(pair_count)
        ])
        low = -jnp.einsum("pij,pjk,pkl->pil", second_inv, below, first_inv, precision=lax.Precision.HIGHEST)
        top = jnp.concatenate([first_inv, jnp.zeros_like(first_inv)], axis=2)
        bottom = jnp.concatenate([low, second_inv], axis=2)
        inv = jnp.concatenate([top, bottom], axis=1)
        size *= 2
    return inv[0]


def local(green, arrival, row_gauge, row_time, damping, trail):
    row_count = lax.axis_size("row")
    col_count = lax.axis_size("col")
    row_pos = lax.axis_index("row")
    col_pos = lax.axis_index("col")
    kq_rows, tile_rows, tile_width = green.shape
    panel_tiles = PANEL // NB
    far_slots = trail.shape[2]
    arrive = arrival[row_gauge][:, :, 0]
    is_live = row_time[:, None] >= arrive
    masked = jnp.where(is_live[:, :, None], green, jnp.zeros_like(green))
    flat_green = masked.reshape(kq_rows, tile_rows * tile_width)

    panel_holds = np.zeros((row_count, col_count), dtype=bool)
    panel_holds[:panel_tiles, :] = True
    panel_piece = spread_share(
        masked[:, 0, :], panel_holds, [[12, 48], [48, 12], [4, 16], [16, 4]], row_count, col_count
    )
    panel_pair = gather_share(panel_piece, (2,), row_count, col_count)
    panel_stack = gather_share(panel_pair, (1,), row_count, col_count)
    panel_cols = jnp.transpose(panel_stack, (2, 1, 0, 3)).reshape(kq_rows, PANEL)

    if col_count == 4:
        col_masks = (1, 3)
    else:
        col_masks = tuple(1 << b for b in range(col_count.bit_length() - 1))
    contract_rows = (((0,), (0,)), ((), ()))
    half = PANEL // 2
    core_bit = row_pos % 2
    diag_part = lax.dot_general(
        lax.dynamic_slice_in_dim(panel_cols, core_bit * half, half, 1),
        panel_cols, contract_rows, preferred_element_type=jnp.float32,
    )
    partial_value = lax.dot_general(
        flat_green, panel_cols, contract_rows, preferred_element_type=jnp.float32
    )
    both_rows = jnp.concatenate([diag_part, partial_value[:tile_width]])
    for col_mask in col_masks:
        col_pairs = [
            (r * col_count + c, r * col_count + (c ^ col_mask))
            for r in range(row_count)
            for c in range(col_count)
        ]
        both_rows = both_rows + lax.ppermute(both_rows, ("row", "col"), col_pairs)
    diag_half = both_rows[:half]
    head_rows = both_rows[half:]
    swap_pairs = [
        (r * col_count + c, (r ^ 1) * col_count + c)
        for r in range(row_count)
        for c in range(col_count)
    ]
    other_half = lax.ppermute(diag_half, ("row", "col"), swap_pairs)
    diag_block = jnp.where(
        core_bit == 0,
        jnp.concatenate([diag_half, other_half]),
        jnp.concatenate([other_half, diag_half]),
    )
    diag_block, rest_rows = lax.optimization_barrier((diag_block, partial_value[tile_width:]))
    rest_sum = rest_rows

    far_holds = np.zeros((row_count, col_count), dtype=bool)
    for slot_no in range(far_slots):
        for c in range(col_count):
            far_holds[panel_tiles + slot_no * col_count + c, c] = True
    far_piece = spread_share(
        head_rows, far_holds, ((32,), (2,), (1,)), row_count, col_count
    )
    by_inverse = (((1,), (1,)), ((), ()))
    unit = jnp.eye(tile_width, dtype=jnp.float32)
    trailing = diag_block + jnp.diag(damping)
    factor_cols = []
    inv_diag = []
    for step in range(panel_tiles):
        head = trailing[:tile_width, :tile_width]
        head_factor = jnp.tril(jnp.linalg.cholesky(head))
        head_inv = lax.linalg.triangular_solve(head_factor, unit, left_side=True, lower=True)
        inv_diag.append(head_inv)
        if step + 1 < panel_tiles:
            panel = lax.dot_general(
                trailing[tile_width:, :tile_width], head_inv, by_inverse,
                precision=lax.Precision.HIGHEST, preferred_element_type=jnp.float32,
            )
            trailing = trailing[tile_width:, tile_width:] - lax.dot_general(
                panel, panel, by_inverse,
                precision=lax.Precision.HIGHEST, preferred_element_type=jnp.float32,
            )
            factor_cols.append(jnp.concatenate([head_factor, panel]))
        else:
            factor_cols.append(head_factor)
        if step < len(col_masks):
            trailing, far_piece, rest_sum = lax.optimization_barrier((trailing, far_piece, rest_sum))
            col_mask = col_masks[step]
            col_pairs = [
                (r * col_count + c, r * col_count + (c ^ col_mask))
                for r in range(row_count)
                for c in range(col_count)
            ]
            rest_sum = rest_sum + lax.ppermute(rest_sum, ("row", "col"), col_pairs)
        if step == 0:
            far_quad = gather_share(far_piece, (4, 8), row_count, col_count)
        if step == 2:
            trailing, far_quad, rest_sum = lax.optimization_barrier((trailing, far_quad, rest_sum))
            far_shared = gather_share(far_quad, (16,), row_count, col_count).reshape(
                far_slots, tile_width, PANEL
            )
    factor = jnp.concatenate(
        [jnp.pad(col, ((step * tile_width, 0), (0, 0))) for step, col in enumerate(factor_cols)],
        axis=1,
    )
    factor_inv = lower_inverse_from_blocks(factor, inv_diag, tile_width)
    factor_inv, far_shared = lax.optimization_barrier((factor_inv, far_shared))
    normal_rows = jnp.concatenate([head_rows, rest_sum])
    far_normal = jnp.roll(far_shared, -1, axis=0).reshape(far_slots * tile_width, PANEL)
    solved = lax.dot_general(
        normal_rows, factor_inv, by_inverse,
        precision=lax.Precision.HIGH, preferred_element_type=jnp.float32,
    )
    far_rows = lax.dot_general(
        far_normal, factor_inv, by_inverse,
        precision=lax.Precision.HIGH, preferred_element_type=jnp.float32,
    )
    solved = solved.reshape(tile_rows, tile_width, PANEL)
    tiles_list = []
    for local_no in range(tile_rows):
        tile_id = local_no * row_count + row_pos
        diag_rows = lax.dynamic_slice_in_dim(
            factor, jnp.minimum(tile_id, panel_tiles - 1) * tile_width, tile_width, 0
        )
        tiles_list.append(jnp.where(tile_id < panel_tiles, diag_rows, solved[local_no]))
    lower_rows = jnp.stack(tiles_list)
    col_share = PANEL // col_count
    chol_out = lax.dynamic_slice_in_dim(lower_rows, col_pos * col_share, col_share, 2)

    update = lax.dot_general(
        lower_rows.reshape(tile_rows * tile_width, PANEL),
        far_rows,
        (((1,), (1,)), ((), ())),
        precision=lax.Precision.HIGH,
        preferred_element_type=jnp.float32,
    )
    update = update.reshape(tile_rows, tile_width, far_slots, tile_width)
    tile_ids = jnp.arange(tile_rows, dtype=jnp.int32) * row_count + row_pos
    below_panel = (tile_ids >= panel_tiles)[:, None, None, None]
    return (chol_out, trail - jnp.where(below_panel, update, jnp.zeros_like(update)))


def solution(mesh):
    return jax.shard_map(
        local,
        mesh=mesh,
        in_specs=(
            P("col", None, "row"),
            P(None, None, "row"),
            P("col"),
            P("col"),
            P(),
            P(None, "row", None, "col"),
        ),
        out_specs=(P(None, "row", "col"), P(None, "row", None, "col")),
        check_vma=False,
    )
```

```python
import numpy as np
import jax
import jax.numpy as jnp
from jax import lax
from jax.sharding import PartitionSpec as P

NB = 128
PANEL = 512


def span_of(masks):
    values = [0]
    for mask in masks:
        values = values + [v ^ mask for v in values]
    return values


def spread_share(piece, holds, spread_rounds, row_count, col_count):
    row_pos = lax.axis_index("row")
    col_pos = lax.axis_index("col")
    flat_pos = row_pos * col_count + col_pos
    have = np.array(holds, dtype=bool)
    for round_masks in spread_rounds:
        gets_all = np.zeros_like(have)
        moved_list = []
        if isinstance(round_masks, list):
            mask_sets = [round_masks]
        else:
            mask_sets = [[mask, mask] for mask in span_of(round_masks)[1:]]
        for parity_masks in mask_sets:
            pairs = []
            gets = np.zeros_like(have)
            for r in range(row_count):
                mask = parity_masks[r % 2]
                for c in range(col_count):
                    if have[r, c] and not have[r ^ mask, c]:
                        pairs.append((r * col_count + c, (r ^ mask) * col_count + c))
                        gets[r ^ mask, c] = True
            assert not (gets & gets_all).any()
            gets_all = gets_all | gets
            moved_list.append((lax.ppermute(piece, ("row", "col"), pairs), gets))
        for moved, gets in moved_list:
            took = jnp.asarray(gets.reshape(-1))[flat_pos]
            piece = jnp.where(took, moved, piece)
        have = have | gets_all
    assert have.all()
    return piece


def gather_share(piece, gather_masks, row_count, col_count):
    row_pos = lax.axis_index("row")
    offsets = span_of(gather_masks)
    recv = [piece]
    for mask in offsets[1:]:
        pairs = [
            (r * col_count + c, (r ^ mask) * col_count + c)
            for r in range(row_count)
            for c in range(col_count)
        ]
        recv.append(lax.ppermute(piece, ("row", "col"), pairs))
    stacked = jnp.stack(recv)
    own_value = sum(
        jnp.where((row_pos & mask) != 0, 1 << bit, 0) for bit, mask in enumerate(gather_masks)
    )
    return jnp.stack(
        [lax.dynamic_index_in_dim(stacked, u ^ own_value, 0, keepdims=False) for u in range(len(offsets))]
    )


def lower_inverse_from_blocks(factor, inv_diag, nb):
    inv = jnp.stack(inv_diag)
    size = nb
    while inv.shape[0] > 1:
        pair_count = inv.shape[0] // 2
        first_inv = inv[0::2]
        second_inv = inv[1::2]
        below = jnp.stack([
            factor[(2 * p + 1) * size:(2 * p + 2) * size, 2 * p * size:(2 * p + 1) * size]
            for p in range(pair_count)
        ])
        low = -jnp.einsum("pij,pjk,pkl->pil", second_inv, below, first_inv, precision=lax.Precision.HIGHEST)
        top = jnp.concatenate([first_inv, jnp.zeros_like(first_inv)], axis=2)
        bottom = jnp.concatenate([low, second_inv], axis=2)
        inv = jnp.concatenate([top, bottom], axis=1)
        size *= 2
    return inv[0]


def local(green, arrival, row_gauge, row_time, damping, trail):
    row_count = lax.axis_size("row")
    col_count = lax.axis_size("col")
    row_pos = lax.axis_index("row")
    col_pos = lax.axis_index("col")
    kq_rows, tile_rows, tile_width = green.shape
    panel_tiles = PANEL // NB
    far_slots = trail.shape[2]
    gauge_count = arrival.shape[0]
    pick = (row_gauge[:, None] == jnp.arange(gauge_count, dtype=row_gauge.dtype)[None, :]).astype(jnp.float32)
    arrive = jnp.dot(
        pick, arrival[:, :, 0].astype(jnp.float32),
        precision=lax.Precision.HIGHEST, preferred_element_type=jnp.float32,
    )
    is_live = row_time[:, None].astype(jnp.float32) >= arrive
    masked = jnp.where(is_live[:, :, None], green, jnp.zeros_like(green))
    flat_green = masked.reshape(kq_rows, tile_rows * tile_width)

    panel_holds = np.zeros((row_count, col_count), dtype=bool)
    panel_holds[:panel_tiles, :] = True
    panel_piece = spread_share(
        masked[:, 0, :], panel_holds, [[12, 48], [48, 12], [4, 16], [16, 4]], row_count, col_count
    )
    panel_pair = gather_share(panel_piece, (2,), row_count, col_count)
    panel_stack = gather_share(panel_pair, (1,), row_count, col_count)
    panel_cols = jnp.transpose(panel_stack, (2, 1, 0, 3)).reshape(kq_rows, PANEL)

    if col_count == 4:
        col_masks = (1, 3)
    else:
        col_masks = tuple(1 << b for b in range(col_count.bit_length() - 1))
    contract_rows = (((0,), (0,)), ((), ()))
    half = PANEL // 2
    core_bit = row_pos % 2
    diag_part = lax.dot_general(
        lax.dynamic_slice_in_dim(panel_cols, core_bit * half, half, 1),
        panel_cols, contract_rows, preferred_element_type=jnp.float32,
    )
    partial_value = lax.dot_general(
        flat_green, panel_cols, contract_rows, preferred_element_type=jnp.float32
    )
    diag_half = diag_part
    for col_mask in col_masks:
        col_pairs = [
            (r * col_count + c, r * col_count + (c ^ col_mask))
            for r in range(row_count)
            for c in range(col_count)
        ]
        diag_half = diag_half + lax.ppermute(diag_half, ("row", "col"), col_pairs)
    swap_pairs = [
        (r * col_count + c, (r ^ 1) * col_count + c)
        for r in range(row_count)
        for c in range(col_count)
    ]
    other_half = lax.ppermute(diag_half, ("row", "col"), swap_pairs)
    diag_block = jnp.where(
        core_bit == 0,
        jnp.concatenate([diag_half, other_half]),
        jnp.concatenate([other_half, diag_half]),
    )
    head_rows = partial_value[:tile_width]
    for col_mask in col_masks:
        col_pairs = [
            (r * col_count + c, r * col_count + (c ^ col_mask))
            for r in range(row_count)
            for c in range(col_count)
        ]
        head_rows = head_rows + lax.ppermute(head_rows, ("row", "col"), col_pairs)
    diag_block, rest_rows = lax.optimization_barrier((diag_block, partial_value[tile_width:]))
    rest_sum = rest_rows

    far_holds = np.zeros((row_count, col_count), dtype=bool)
    for slot_no in range(far_slots):
        for c in range(col_count):
            far_holds[panel_tiles + slot_no * col_count + c, c] = True
    far_piece = spread_share(
        head_rows, far_holds, ((32,), (2,), (1,)), row_count, col_count
    )
    by_inverse = (((1,), (1,)), ((), ()))
    unit = jnp.eye(tile_width, dtype=jnp.float32)
    trailing = diag_block + jnp.diag(damping)
    factor_cols = []
    inv_diag = []
    for step in range(panel_tiles):
        head = trailing[:tile_width, :tile_width]
        head_factor = jnp.tril(jnp.linalg.cholesky(head))
        head_inv = lax.linalg.triangular_solve(head_factor, unit, left_side=True, lower=True)
        inv_diag.append(head_inv)
        if step + 1 < panel_tiles:
            panel = lax.dot_general(
                trailing[tile_width:, :tile_width], head_inv, by_inverse,
                precision=lax.Precision.HIGHEST, preferred_element_type=jnp.float32,
            )
            trailing = trailing[tile_width:, tile_width:] - lax.dot_general(
                panel, panel, by_inverse,
                precision=lax.Precision.HIGHEST, preferred_element_type=jnp.float32,
            )
            factor_cols.append(jnp.concatenate([head_factor, panel]))
        else:
            factor_cols.append(head_factor)
        if step < len(col_masks):
            trailing, far_piece, rest_sum = lax.optimization_barrier((trailing, far_piece, rest_sum))
            col_mask = col_masks[step]
            col_pairs = [
                (r * col_count + c, r * col_count + (c ^ col_mask))
                for r in range(row_count)
                for c in range(col_count)
            ]
            rest_sum = rest_sum + lax.ppermute(rest_sum, ("row", "col"), col_pairs)
        if step == 0:
            far_quad = gather_share(far_piece, (4, 8), row_count, col_count)
        if step == 2:
            trailing, far_quad, rest_sum = lax.optimization_barrier((trailing, far_quad, rest_sum))
            far_shared = gather_share(far_quad, (16,), row_count, col_count).reshape(
                far_slots, tile_width, PANEL
            )
    factor = jnp.concatenate(
        [jnp.pad(col, ((step * tile_width, 0), (0, 0))) for step, col in enumerate(factor_cols)],
        axis=1,
    )
    factor_inv = lower_inverse_from_blocks(factor, inv_diag, tile_width)
    factor_inv, far_shared = lax.optimization_barrier((factor_inv, far_shared))
    normal_rows = jnp.concatenate([head_rows, rest_sum])
    far_normal = jnp.roll(far_shared, -1, axis=0).reshape(far_slots * tile_width, PANEL)
    solved = lax.dot_general(
        normal_rows, factor_inv, by_inverse,
        precision=lax.Precision.HIGH, preferred_element_type=jnp.float32,
    )
    far_rows = lax.dot_general(
        far_normal, factor_inv, by_inverse,
        precision=lax.Precision.HIGH, preferred_element_type=jnp.float32,
    )
    solved = solved.reshape(tile_rows, tile_width, PANEL)
    tiles_list = []
    for local_no in range(tile_rows):
        tile_id = local_no * row_count + row_pos
        diag_rows = lax.dynamic_slice_in_dim(
            factor, jnp.minimum(tile_id, panel_tiles - 1) * tile_width, tile_width, 0
        )
        tiles_list.append(jnp.where(tile_id < panel_tiles, diag_rows, solved[local_no]))
    lower_rows = jnp.stack(tiles_list)
    col_share = PANEL // col_count
    chol_out = lax.dynamic_slice_in_dim(lower_rows, col_pos * col_share, col_share, 2)

    update = lax.dot_general(
        lower_rows.reshape(tile_rows * tile_width, PANEL),
        far_rows,
        (((1,), (1,)), ((), ())),
        precision=lax.Precision.HIGH,
        preferred_element_type=jnp.float32,
    )
    update = update.reshape(tile_rows, tile_width, far_slots, tile_width)
    tile_ids = jnp.arange(tile_rows, dtype=jnp.int32) * row_count + row_pos
    below_panel = (tile_ids >= panel_tiles)[:, None, None, None]
    return (chol_out, trail - jnp.where(below_panel, update, jnp.zeros_like(update)))


def solution(mesh):
    return jax.shard_map(
        local,
        mesh=mesh,
        in_specs=(
            P("col", None, "row"),
            P(None, None, "row"),
            P("col"),
            P("col"),
            P(),
            P(None, "row", None, "col"),
        ),
        out_specs=(P(None, "row", "col"), P(None, "row", None, "col")),
        check_vma=False,
    )
```

```python
import numpy as np
import jax
import jax.numpy as jnp
from jax import lax
from jax.sharding import PartitionSpec as P

NB = 128
PANEL = 512


def span_of(masks):
    values = [0]
    for mask in masks:
        values = values + [v ^ mask for v in values]
    return values


def spread_share(piece, holds, spread_rounds, row_count, col_count):
    row_pos = lax.axis_index("row")
    col_pos = lax.axis_index("col")
    flat_pos = row_pos * col_count + col_pos
    have = np.array(holds, dtype=bool)
    for round_masks in spread_rounds:
        gets_all = np.zeros_like(have)
        moved_list = []
        if isinstance(round_masks, list):
            mask_sets = [round_masks]
        else:
            mask_sets = [[mask, mask] for mask in span_of(round_masks)[1:]]
        for parity_masks in mask_sets:
            pairs = []
            gets = np.zeros_like(have)
            for r in range(row_count):
                mask = parity_masks[r % 2]
                for c in range(col_count):
                    if have[r, c] and not have[r ^ mask, c]:
                        pairs.append((r * col_count + c, (r ^ mask) * col_count + c))
                        gets[r ^ mask, c] = True
            assert not (gets & gets_all).any()
            gets_all = gets_all | gets
            moved_list.append((lax.ppermute(piece, ("row", "col"), pairs), gets))
        for moved, gets in moved_list:
            took = jnp.asarray(gets.reshape(-1))[flat_pos]
            piece = jnp.where(took, moved, piece)
        have = have | gets_all
    assert have.all()
    return piece


def gather_share(piece, gather_masks, row_count, col_count):
    row_pos = lax.axis_index("row")
    offsets = span_of(gather_masks)
    recv = [piece]
    for mask in offsets[1:]:
        pairs = [
            (r * col_count + c, (r ^ mask) * col_count + c)
            for r in range(row_count)
            for c in range(col_count)
        ]
        recv.append(lax.ppermute(piece, ("row", "col"), pairs))
    stacked = jnp.stack(recv)
    own_value = sum(
        jnp.where((row_pos & mask) != 0, 1 << bit, 0) for bit, mask in enumerate(gather_masks)
    )
    return jnp.stack(
        [lax.dynamic_index_in_dim(stacked, u ^ own_value, 0, keepdims=False) for u in range(len(offsets))]
    )


def lower_inverse_from_blocks(factor, inv_diag, nb):
    inv = jnp.stack(inv_diag)
    size = nb
    while inv.shape[0] > 1:
        pair_count = inv.shape[0] // 2
        first_inv = inv[0::2]
        second_inv = inv[1::2]
        below = jnp.stack([
            factor[(2 * p + 1) * size:(2 * p + 2) * size, 2 * p * size:(2 * p + 1) * size]
            for p in range(pair_count)
        ])
        low = -jnp.einsum("pij,pjk,pkl->pil", second_inv, below, first_inv, precision=lax.Precision.HIGHEST)
        top = jnp.concatenate([first_inv, jnp.zeros_like(first_inv)], axis=2)
        bottom = jnp.concatenate([low, second_inv], axis=2)
        inv = jnp.concatenate([top, bottom], axis=1)
        size *= 2
    return inv[0]


def local(green, arrival, row_gauge, row_time, damping, trail):
    row_count = lax.axis_size("row")
    col_count = lax.axis_size("col")
    row_pos = lax.axis_index("row")
    col_pos = lax.axis_index("col")
    kq_rows, tile_rows, tile_width = green.shape
    panel_tiles = PANEL // NB
    far_slots = trail.shape[2]
    arrive = arrival[row_gauge][:, :, 0]
    is_live = row_time[:, None] >= arrive
    masked = jnp.where(is_live[:, :, None], green, jnp.zeros_like(green))
    flat_green = masked.reshape(kq_rows, tile_rows * tile_width)

    panel_holds = np.zeros((row_count, col_count), dtype=bool)
    panel_holds[:panel_tiles, :] = True
    panel_piece = spread_share(
        masked[:, 0, :], panel_holds, [[12, 48], [48, 12], [4, 16], [16, 4]], row_count, col_count
    )
    panel_pair = gather_share(panel_piece, (2,), row_count, col_count)
    panel_stack = gather_share(panel_pair, (1,), row_count, col_count)
    panel_cols = jnp.transpose(panel_stack, (2, 1, 0, 3)).reshape(kq_rows, PANEL)

    if col_count == 4:
        col_masks = (1, 3)
    else:
        col_masks = tuple(1 << b for b in range(col_count.bit_length() - 1))
    contract_rows = (((0,), (0,)), ((), ()))
    half = PANEL // 2
    core_bit = row_pos % 2
    diag_part = lax.dot_general(
        lax.dynamic_slice_in_dim(panel_cols, core_bit * half, half, 1),
        panel_cols, contract_rows, preferred_element_type=jnp.float32,
    )
    partial_value = lax.dot_general(
        flat_green, panel_cols, contract_rows, preferred_element_type=jnp.float32
    )
    diag_half = diag_part
    for col_mask in col_masks:
        col_pairs = [
            (r * col_count + c, r * col_count + (c ^ col_mask))
            for r in range(row_count)
            for c in range(col_count)
        ]
        diag_half = diag_half + lax.ppermute(diag_half, ("row", "col"), col_pairs)
    swap_pairs = [
        (r * col_count + c, (r ^ 1) * col_count + c)
        for r in range(row_count)
        for c in range(col_count)
    ]
    other_half = lax.ppermute(diag_half, ("row", "col"), swap_pairs)
    diag_block = jnp.where(
        core_bit == 0,
        jnp.concatenate([diag_half, other_half]),
        jnp.concatenate([other_half, diag_half]),
    )
    head_rows = partial_value[:tile_width]
    for col_mask in col_masks:
        col_pairs = [
            (r * col_count + c, r * col_count + (c ^ col_mask))
            for r in range(row_count)
            for c in range(col_count)
        ]
        head_rows = head_rows + lax.ppermute(head_rows, ("row", "col"), col_pairs)
    diag_block, rest_rows = lax.optimization_barrier((diag_block, partial_value[tile_width:]))
    rest_sum = rest_rows

    far_holds = np.zeros((row_count, col_count), dtype=bool)
    for slot_no in range(far_slots):
        for c in range(col_count):
            far_holds[panel_tiles + slot_no * col_count + c, c] = True
    far_piece = spread_share(
        head_rows, far_holds, ((32,), (1, 2)), row_count, col_count
    )
    by_inverse = (((1,), (1,)), ((), ()))
    unit = jnp.eye(tile_width, dtype=jnp.float32)
    trailing = diag_block + jnp.diag(damping)
    factor_cols = []
    inv_diag = []
    for step in range(panel_tiles):
        head = trailing[:tile_width, :tile_width]
        head_factor = jnp.tril(jnp.linalg.cholesky(head))
        head_inv = lax.linalg.triangular_solve(head_factor, unit, left_side=True, lower=True)
        inv_diag.append(head_inv)
        if step + 1 < panel_tiles:
            panel = lax.dot_general(
                trailing[tile_width:, :tile_width], head_inv, by_inverse,
                precision=lax.Precision.HIGHEST, preferred_element_type=jnp.float32,
            )
            trailing = trailing[tile_width:, tile_width:] - lax.dot_general(
                panel, panel, by_inverse,
                precision=lax.Precision.HIGHEST, preferred_element_type=jnp.float32,
            )
            factor_cols.append(jnp.concatenate([head_factor, panel]))
        else:
            factor_cols.append(head_factor)
        if step < len(col_masks):
            trailing, far_piece, rest_sum = lax.optimization_barrier((trailing, far_piece, rest_sum))
            col_mask = col_masks[step]
            col_pairs = [
                (r * col_count + c, r * col_count + (c ^ col_mask))
                for r in range(row_count)
                for c in range(col_count)
            ]
            rest_sum = rest_sum + lax.ppermute(rest_sum, ("row", "col"), col_pairs)
        if step == 0:
            far_quad = gather_share(far_piece, (4, 8), row_count, col_count)
        if step == 2:
            trailing, far_quad, rest_sum = lax.optimization_barrier((trailing, far_quad, rest_sum))
            far_shared = gather_share(far_quad, (16,), row_count, col_count).reshape(
                far_slots, tile_width, PANEL
            )
    factor = jnp.concatenate(
        [jnp.pad(col, ((step * tile_width, 0), (0, 0))) for step, col in enumerate(factor_cols)],
        axis=1,
    )
    factor_inv = lower_inverse_from_blocks(factor, inv_diag, tile_width)
    factor_inv, far_shared = lax.optimization_barrier((factor_inv, far_shared))
    normal_rows = jnp.concatenate([head_rows, rest_sum])
    far_normal = jnp.roll(far_shared, -1, axis=0).reshape(far_slots * tile_width, PANEL)
    solved = lax.dot_general(
        normal_rows, factor_inv, by_inverse,
        precision=lax.Precision.HIGH, preferred_element_type=jnp.float32,
    )
    far_rows = lax.dot_general(
        far_normal, factor_inv, by_inverse,
        precision=lax.Precision.HIGH, preferred_element_type=jnp.float32,
    )
    solved = solved.reshape(tile_rows, tile_width, PANEL)
    tiles_list = []
    for local_no in range(tile_rows):
        tile_id = local_no * row_count + row_pos
        diag_rows = lax.dynamic_slice_in_dim(
            factor, jnp.minimum(tile_id, panel_tiles - 1) * tile_width, tile_width, 0
        )
        tiles_list.append(jnp.where(tile_id < panel_tiles, diag_rows, solved[local_no]))
    lower_rows = jnp.stack(tiles_list)
    col_share = PANEL // col_count
    chol_out = lax.dynamic_slice_in_dim(lower_rows, col_pos * col_share, col_share, 2)

    update = lax.dot_general(
        lower_rows.reshape(tile_rows * tile_width, PANEL),
        far_rows,
        (((1,), (1,)), ((), ())),
        precision=lax.Precision.HIGH,
        preferred_element_type=jnp.float32,
    )
    update = update.reshape(tile_rows, tile_width, far_slots, tile_width)
    tile_ids = jnp.arange(tile_rows, dtype=jnp.int32) * row_count + row_pos
    below_panel = (tile_ids >= panel_tiles)[:, None, None, None]
    return (chol_out, trail - jnp.where(below_panel, update, jnp.zeros_like(update)))


def solution(mesh):
    return jax.shard_map(
        local,
        mesh=mesh,
        in_specs=(
            P("col", None, "row"),
            P(None, None, "row"),
            P("col"),
            P("col"),
            P(),
            P(None, "row", None, "col"),
        ),
        out_specs=(P(None, "row", "col"), P(None, "row", None, "col")),
        check_vma=False,
    )
```
